256 devices in a mesh: gy: 8 (over y_lo, x), gz: 32 (over y_hi, z, core).
Axes of the slice: x: 4, y: 4 (y_hi: 2, y_lo: 2; y = y_hi * 2 + y_lo), z: 8, core: 2. Of those that a mesh axis runs over, the one named last changes fastest.
Arguments:
- velocity_modes: float32 [3, 64, 512, 576], P(None, None, 'gy', 'gz'), may hold values from -0.36 to 0.36
- conformation: float32 [6, 64, 512, 1152], P(None, 'gz', 'gy'), may hold values from -0.5 to 16, as said below
Outputs:
- conformation_next: float32 [6, 64, 512, 1152], P(None, 'gz', 'gy')
- stress_modes: float32 [3, 64, 512, 576], P(None, None, 'gy', 'gz')
The draws below stay inside these ranges and needn't reach their ends.
Inputs may be any that keep to these rules, and one draw needn't show every extreme that they name: `conformation`: components 0, 3 and 5 (the diagonal) lie in 1 to 16 and the others in -0.5 to 0.5, so the trace is at most 48.
All inputs are finite; a program needn't handle non-finite values.
Results may differ from the reference program's by a relative error of at most 0.0003.
Values sent between devices are 32-bit elements; how exact they have to be, the bound alone decides.
A program may use at most 128 MiB of HBM per device.

```python
import math
import jax
import jax.numpy as jnp
from jax import lax

KZ = 576
NZF = 1152
NYF = 512
PLANES = 64


def draw_conformation(key, part):
    shape = (PLANES, NYF, NZF)
    keys = jax.random.split(key, 6)
    diagonal = [jnp.minimum(jnp.exp(jax.random.uniform(keys[i], shape, jnp.float32, 0.0, math.log(16.0))), 16.0) for i in range(3)]
    offdiag = [jax.random.uniform(keys[3 + i], shape, jnp.float32, -0.5, 0.5) for i in range(3)]
    return jnp.stack([diagonal[0], offdiag[0], offdiag[1], diagonal[1], offdiag[2], diagonal[2]])


def shard_levels(stream_key, extent, cuts, smallest, largest):
    def one(axis_at, parts):
        steps = jax.random.uniform(jax.random.fold_in(jax.random.fold_in(stream_key, 6), axis_at), (parts,), jnp.float32, smallest / len(cuts), largest / len(cuts))
        return jnp.repeat(jnp.exp(steps), extent[axis_at] // parts).reshape((-1,) + (1,) * (len(extent) - axis_at - 1))

    level = one(*cuts[0])
    for cut in cuts[1:]:
        level = level * one(*cut)
    return level


def bell_draw(key, extent, width, bound, pieces=(), held_as=jnp.bfloat16):
    gain = shard_levels(key, extent, pieces, -0.22, 0.18) if pieces else 1.0
    values = jax.random.normal(key, extent, jnp.float32) * width * gain
    return jnp.minimum(jnp.maximum(values, -bound), bound).astype(held_as)


def setup_inputs(seed: int = 0) -> dict:
    streams_of = jax.random.split(jax.random.key(seed), 3)
    velocity_modes = bell_draw(streams_of[0], (3, PLANES, NYF, KZ), 0.06, 0.36, ((2, 8), (3, 32)), jnp.float32)
    conformation = draw_conformation(jax.random.fold_in(streams_of[2], 71), 0)
    return dict(velocity_modes=velocity_modes, conformation=conformation)


max_extension = 60.0
time_step = 0.25
relax_time = 4.0
stress_scale = 0.2
component_index = ((0, 1, 2), (1, 3, 4), (2, 4, 5))


def spanwise_tables(modes, points):
    half = modes // 2
    index_j = jnp.arange(modes, dtype=jnp.int32)
    index_n = jnp.arange(points, dtype=jnp.int32)
    wave = jnp.where(index_j < half, index_j, index_j - half + 1)
    phase = (wave[:, None] * index_n[None, :]) % points
    theta = phase.astype(jnp.float32) * (2.0 * math.pi / points)
    rate = (wave.astype(jnp.float32) * (2.0 * math.pi / points))[:, None]
    is_cosine = (index_j < half)[:, None]
    basis = jnp.where(is_cosine, jnp.cos(theta), jnp.sin(theta))
    slope = jnp.where(is_cosine, -rate * jnp.sin(theta), rate * jnp.cos(theta))
    weight = jnp.where(index_j == 0, 1.0 / points, 2.0 / points).astype(jnp.float32)
    return basis, slope, weight


def trace_factor(conf):
    return (max_extension - 3.0) / (max_extension - (conf[0] + conf[3] + conf[5]))


def upwind(speed, behind, ahead):
    return jnp.maximum(speed, 0.0) * behind + jnp.minimum(speed, 0.0) * ahead


def advance(conf_p, conf_y, vel_p, vel_y, vel_dz, project, project_dz):
    highest = lax.Precision.HIGHEST
    conf = conf_p[:, 1:-1]
    vel = vel_p[:, 1:-1]
    factor = trace_factor(conf)
    pulled_p = conf_p * trace_factor(conf_p)[None]
    pulled_y = conf_y * trace_factor(conf_y)[None]
    grad_x = (vel_p[:, 2:] - vel_p[:, :-2]) * 0.5
    grad_y = (vel_y[:, :, 2:] - vel_y[:, :, :-2]) * 0.5
    slopes = (grad_x, grad_y, vel_dz)
    transport = upwind(vel[0][None], conf - conf_p[:, :-2], conf_p[:, 2:] - conf)
    transport = transport + upwind(vel[1][None], conf - conf_y[:, :, :-2], conf_y[:, :, 2:] - conf)
    transport = transport + upwind(vel[2][None], conf - jnp.roll(conf, 1, axis=3), jnp.roll(conf, -1, axis=3) - conf)
    entries = []
    for first, second in ((0, 0), (0, 1), (0, 2), (1, 1), (1, 2), (2, 2)):
        terms = [slopes[k][first] * conf[component_index[k][second]] + conf[component_index[first][k]] * slopes[k][second] for k in range(3)]
        entries.append(terms[0] + terms[1] + terms[2])
    stretch = jnp.stack(entries)
    identity = jnp.array([1.0, 0.0, 0.0, 1.0, 0.0, 1.0], dtype=jnp.float32)[:, None, None, None]
    relaxed = factor[None] * conf - identity
    updated = conf + time_step * (stretch - transport - relaxed / relax_time)
    along = []
    spanwise = []
    for row in range(3):
        first = pulled_p[component_index[row][0]]
        second = pulled_y[component_index[row][1]]
        along.append(stress_scale * ((first[2:] - first[:-2]) * 0.5 + (second[:, 2:] - second[:, :-2]) * 0.5))
        spanwise.append(stress_scale * pulled_p[component_index[row][2], 1:-1])
    along = jnp.stack(along)
    spanwise = jnp.stack(spanwise)
    modes = jnp.einsum('cpyn,nk->cpyk', along, project, precision=highest)
    modes = modes + jnp.einsum('cpyn,nk->cpyk', spanwise, project_dz, precision=highest)
    return updated, modes


def reference(velocity_modes, conformation):
    highest = lax.Precision.HIGHEST
    basis, slope, weight = spanwise_tables(KZ, NZF)
    project = (basis * weight[:, None]).T
    project_dz = -(slope * weight[:, None]).T
    fine = jnp.einsum('cpyk,kn->cpyn', velocity_modes, basis, precision=highest)
    fine_dz = jnp.einsum('cpyk,kn->cpyn', velocity_modes, slope, precision=highest)

    def one_plane(plane):
        rows = jnp.stack([(plane - 1) % PLANES, plane, (plane + 1) % PLANES]).astype(jnp.int32)
        conf_p = jnp.take(conformation, rows, axis=1)
        vel_p = jnp.take(fine, rows, axis=1)
        centre_conf = lax.dynamic_slice_in_dim(conformation, plane, 1, 1)
        centre_vel = lax.dynamic_slice_in_dim(fine, plane, 1, 1)
        vel_dz = lax.dynamic_slice_in_dim(fine_dz, plane, 1, 1)
        widths = ((0, 0), (0, 0), (1, 1), (0, 0))
        conf_y = jnp.pad(centre_conf, widths)
        vel_y = jnp.pad(centre_vel, widths)
        updated, modes = advance(conf_p, conf_y, vel_p, vel_y, vel_dz, project, project_dz)
        return updated[:, 0], modes[:, 0]

    updated, modes = lax.map(one_plane, jnp.arange(PLANES, dtype=jnp.int32))
    return jnp.moveaxis(updated, 0, 1), jnp.moveaxis(modes, 0, 1)
```

```python
import functools
import math

import jax
import jax.numpy as jnp
import ml_dtypes
import numpy as np
from jax import lax
from jax.experimental import pallas as pl
from jax.experimental.pallas import tpu as pltpu
from jax.sharding import PartitionSpec as P

max_extension = 60.0
time_step = 0.25
relax_time = 4.0
stress_scale = 0.2
component_index = ((0, 1, 2), (1, 3, 4), (2, 4, 5))
MESH = pl.DeviceIdType.MESH
edge = 8


def round_up(value, unit):
    return (value + unit - 1) // unit * unit


@functools.lru_cache
def spanwise_tables(modes, points, depth):
    half = modes // 2
    index_j = np.arange(modes, dtype=np.int64)
    index_n = np.arange(points, dtype=np.int64)
    wave = np.where(index_j < half, index_j, index_j - half + 1)
    theta = (wave[:, None] * index_n[None, :] % points) * (2.0 * math.pi / points)
    rate = wave[:, None] * (2.0 * math.pi / points)
    is_cosine = (index_j < half)[:, None]
    basis = np.where(is_cosine, np.cos(theta), np.sin(theta))
    slope = np.where(is_cosine, -rate * np.sin(theta), rate * np.cos(theta))
    tables = []
    for table in (basis, slope):
        table = np.pad(table, ((0, depth - modes), (0, 0))).astype(np.float32)
        head = table.astype(ml_dtypes.bfloat16)
        rest = (table - head.astype(np.float32)).astype(ml_dtypes.bfloat16)
        tables.append(np.concatenate([head, rest], axis=0))
    return tables


def split(value):
    head = value.astype(jnp.bfloat16)
    return head, (value - head.astype(jnp.float32)).astype(jnp.bfloat16)


def kernel(
    dims,
    vm, conf, tab_b, tab_s,
    out, sout,
    vmv, confx, fac, send, recv, osend, orecv, cols, rows, vhalo, yhalo, lhs, velx, veldz,
    nxt, tbv, tsv, pull, res, sbuf,
    load_sem, tab_sem, own_sem, out_sem,
    a2a_send, a2a_recv, o2a_send, o2a_recv,
    cx_send, cx_recv, cy_send, cy_recv, vx_send, vx_recv, vy_send, vy_recv,
):
    ngy, ngz, nm, ny, nz, depth = dims
    modes = nm * ngz
    gy = lax.axis_index("gy")
    gz = lax.axis_index("gz")
    right = lax.rem(gz + 1, ngz)
    left = lax.rem(gz + ngz - 1, ngz)
    has_low = gy > 0
    has_high = gy < ngy - 1
    body = slice(edge, edge + ny)
    f32 = jnp.float32

    load_vm = pltpu.make_async_copy(vm, vmv, load_sem.at[0])
    load_vm.start()
    load_conf = pltpu.make_async_copy(conf, confx.at[:, 1:3, body, :], load_sem.at[1])
    load_conf.start()
    table_loads = []
    for index, (source, target) in enumerate(((tab_b, tbv), (tab_s, tsv))):
        table_loads.append(
            pltpu.make_async_copy(source, target.at[0 : 2 * depth], tab_sem.at[2 * index])
        )
        table_loads.append(
            pltpu.make_async_copy(
                source.at[0:depth], target.at[2 * depth : 3 * depth], tab_sem.at[2 * index + 1]
            )
        )
    for load in table_loads:
        load.start()

    barrier = pltpu.get_barrier_semaphore()

    def greet(step, carry):
        peer = lax.rem(gz + step, ngz)
        pl.semaphore_signal(barrier, inc=1, device_id=(gy, peer), device_id_type=MESH)
        return carry

    lax.fori_loop(1, ngz, greet, 0)

    @pl.when(has_low)
    def _():
        pl.semaphore_signal(barrier, inc=1, device_id=(gy - 1, gz), device_id_type=MESH)

    @pl.when(has_high)
    def _():
        pl.semaphore_signal(barrier, inc=1, device_id=(gy + 1, gz), device_id_type=MESH)

    low_count = lax.div(gy + ngy - 1, ngy)
    high_count = lax.div(2 * ngy - 2 - gy, ngy)
    pl.semaphore_wait(barrier, ngz - 1 + low_count + high_count)

    cx_up = [
        pltpu.make_async_remote_copy(
            conf.at[c, 1], confx.at[c, 0, body, :], cx_send.at[0, c], cx_recv.at[0, c],
            device_id=(gy, right), device_id_type=MESH,
        )
        for c in range(6)
    ]
    cx_down = [
        pltpu.make_async_remote_copy(
            conf.at[c, 0], confx.at[c, 3, body, :], cx_send.at[1, c], cx_recv.at[1, c],
            device_id=(gy, left), device_id_type=MESH,
        )
        for c in range(6)
    ]
    cy_up = pltpu.make_async_remote_copy(
        conf.at[:, :, ny - edge : ny, :], confx.at[:, 1:3, 0:edge, :],
        cy_send.at[0], cy_recv.at[0], device_id=(gy + 1, gz), device_id_type=MESH,
    )
    cy_down = pltpu.make_async_remote_copy(
        conf.at[:, :, 0:edge, :], confx.at[:, 1:3, edge + ny : ny + 2 * edge, :],
        cy_send.at[1], cy_recv.at[1], device_id=(gy - 1, gz), device_id_type=MESH,
    )
    for c in range(6):
        cx_up[c].start()
        cx_down[c].start()

    @pl.when(has_high)
    def _():
        cy_up.start()

    @pl.when(has_low)
    def _():
        cy_down.start()

    load_vm.wait()

    def pack(cm, carry):
        even = vmv[cm, pl.ds(0, ngz, stride=2), :]
        odd = vmv[cm, pl.ds(1, ngz, stride=2), :]
        send[:, cm, :] = jnp.concatenate([even, odd], axis=1)
        return carry

    lax.fori_loop(0, 3 * nm, pack, 0)

    def message(source, target, send_sem, recv_sem, mine, theirs, peer):
        return pltpu.make_async_remote_copy(
            source.at[mine], target.at[theirs], send_sem.at[mine], recv_sem.at[theirs],
            device_id=(gy, peer), device_id_type=MESH,
        )

    def exchange_start(source, target, send_sem, recv_sem, own):
        def start(step, carry):
            peer = lax.rem(gz + step, ngz)
            message(source, target, send_sem, recv_sem, peer, gz, peer).start()
            return carry

        lax.fori_loop(1, ngz, start, 0)
        pltpu.make_async_copy(source.at[gz], target.at[gz], own).start()

    def exchange_recv(source, target, send_sem, recv_sem, own):
        def wait(step, carry):
            peer = lax.rem(gz + ngz - step, ngz)
            message(source, target, send_sem, recv_sem, peer, peer, peer).wait_recv()
            return carry

        pltpu.make_async_copy(source.at[gz], target.at[gz], own).wait()
        lax.fori_loop(1, ngz, wait, 0)

    def exchange_sent(source, target, send_sem, recv_sem):
        def wait(step, carry):
            peer = lax.rem(gz + step, ngz)
            message(source, target, send_sem, recv_sem, peer, peer, peer).wait_send()
            return carry

        lax.fori_loop(1, ngz, wait, 0)

    exchange_start(send, recv, a2a_send, a2a_recv, own_sem.at[0])

    load_conf.wait()
    for load in table_loads:
        load.wait()
    for c in range(6):
        cx_up[c].wait_recv()
        cx_down[c].wait_recv()

    @pl.when(has_low)
    def _():
        cy_up.wait_recv()

    @pl.when(has_high)
    def _():
        cy_down.wait_recv()

    @pl.when(jnp.logical_not(has_low))
    def _():
        confx[:, 1:3, 0:edge, :] = jnp.zeros((6, 2, edge, nz), f32)

    @pl.when(jnp.logical_not(has_high))
    def _():
        confx[:, 1:3, edge + ny : ny + 2 * edge, :] = jnp.zeros((6, 2, edge, nz), f32)

    def factor_rows(plane, first):
        at = pl.ds(first, 8)
        trace = confx[0, plane, at, :] + confx[3, plane, at, :] + confx[5, plane, at, :]
        fac[plane, at, :] = (max_extension - 3.0) / (max_extension - trace)

    def factor_outer(block, carry):
        first = pl.multiple_of(edge + block * 8, 8)
        factor_rows(0, first)
        factor_rows(3, first)
        return carry

    def factor_inner(block, carry):
        first = pl.multiple_of(block * 8, 8)
        factor_rows(1, first)
        factor_rows(2, first)
        return carry

    lax.fori_loop(0, ny // 8, factor_outer, 0)
    lax.fori_loop(0, ny // 8 + 2, factor_inner, 0)

    weight = 2.0 / nz

    def stress_rows(step, carry):
        plane = step // (ny // 16)
        first = pl.multiple_of(edge + (step % (ny // 16)) * 16, 8)
        here = pl.ds(first, 16)
        around = pl.ds(pl.multiple_of(first - 8, 8), 32)
        for row in range(3):
            cx, cy, cz = component_index[row]
            pulled = fac[plane + 1, around, :] * confx[cy, plane + 1, around, :]
            along = (
                fac[plane + 2, here, :] * confx[cx, plane + 2, here, :]
                - fac[plane, here, :] * confx[cx, plane, here, :]
            ) + (pulled[9:25] - pulled[7:23])
            spanwise = fac[plane + 1, here, :] * confx[cz, plane + 1, here, :]
            at = pl.ds(pl.multiple_of(row * 2 * ny + plane * ny + first - edge, 16), 16)
            head, rest = split(along * (0.5 * stress_scale * weight))
            pull[0, at, :] = head
            pull[1, at, :] = rest
            head, rest = split(spanwise * (-stress_scale * weight))
            pull[2, at, :] = head
            pull[3, at, :] = rest
        return carry

    lax.fori_loop(0, 2 * (ny // 16), stress_rows, 0)

    chunk = modes // 2

    def across(a, b):
        return lax.dot_general(a, b, (((1,), (1,)), ((), ())), preferred_element_type=f32)

    def project(step, carry):
        first = pl.multiple_of(step * chunk, 16)
        head = pl.ds(first, chunk)
        rest = pl.ds(pl.multiple_of(depth + first, 16), chunk)
        total = across(tbv[head, :], pull[0]) + across(tsv[head, :], pull[2])
        total = total + (across(tbv[head, :], pull[1]) + across(tsv[head, :], pull[3]))
        total = total + (across(tbv[rest, :], pull[0]) + across(tsv[rest, :], pull[2]))
        res[pl.ds(first, chunk), :] = total
        return carry

    lax.fori_loop(0, 2, project, 0)
    head_row = lax.broadcasted_iota(jnp.int32, (8, 6 * ny), 0) == 0
    res[0:8, :] = jnp.where(head_row, 0.5 * res[0:8, :], res[0:8, :])
    for k in range(ngz):
        for c in range(3):
            osend[k, c * nm : (c + 1) * nm, :] = res[
                k * nm : (k + 1) * nm, c * 2 * ny : (c + 1) * 2 * ny
            ]
    exchange_start(osend, orecv, o2a_send, o2a_recv, own_sem.at[1])

    exchange_recv(send, recv, a2a_send, a2a_recv, own_sem.at[0])
    for c in range(3):
        cols[c, modes:depth, :] = jnp.zeros((depth - modes, 2 * ny), f32)
        for k in range(ngz):
            cols[c, k * nm : (k + 1) * nm, :] = recv[k, c * nm : (c + 1) * nm, :]
        turned = cols[c].T
        rows[c] = turned.reshape(2, ny, depth)

    vx_up = pltpu.make_async_remote_copy(
        rows.at[:, 1], vhalo.at[0], vx_send.at[0], vx_recv.at[0],
        device_id=(gy, right), device_id_type=MESH,
    )
    vx_down = pltpu.make_async_remote_copy(
        rows.at[:, 0], vhalo.at[1], vx_send.at[1], vx_recv.at[1],
        device_id=(gy, left), device_id_type=MESH,
    )
    vy_up = pltpu.make_async_remote_copy(
        rows.at[:, :, ny - edge : ny, :], yhalo.at[0], vy_send.at[0], vy_recv.at[0],
        device_id=(gy + 1, gz), device_id_type=MESH,
    )
    vy_down = pltpu.make_async_remote_copy(
        rows.at[:, :, 0:edge, :], yhalo.at[1], vy_send.at[1], vy_recv.at[1],
        device_id=(gy - 1, gz), device_id_type=MESH,
    )
    vx_up.start()
    vx_down.start()

    @pl.when(has_high)
    def _():
        vy_up.start()

    @pl.when(has_low)
    def _():
        vy_down.start()

    def put_lhs(first, value):
        head, rest = split(value)
        at = slice(first, first + value.shape[0])
        lhs[at, 0:depth] = head
        lhs[at, depth : 2 * depth] = head
        lhs[at, 2 * depth : 3 * depth] = rest

    for c in range(3):
        for p in range(2):
            put_lhs((c * 2 + p) * ny, rows[c, p])

    wide = nz // 3

    def spread_own(step, carry):
        at = pl.ds(pl.multiple_of(step * wide, 128), wide)
        fine = jnp.dot(lhs[0 : 6 * ny, :], tbv[:, at], preferred_element_type=f32)
        velx[:, 1:3, body, at] = fine.reshape(3, 2, ny, wide)
        fine = jnp.dot(lhs[0 : 6 * ny, :], tsv[:, at], preferred_element_type=f32)
        veldz[:, :, :, at] = fine.reshape(3, 2, ny, wide)
        return carry

    lax.fori_loop(0, 3, spread_own, 0)

    vx_up.wait_recv()
    vx_down.wait_recv()

    @pl.when(has_low)
    def _():
        vy_up.wait_recv()

    @pl.when(has_high)
    def _():
        vy_down.wait_recv()

    @pl.when(jnp.logical_not(has_low))
    def _():
        yhalo[0] = jnp.zeros((3, 2, edge, depth), f32)

    @pl.when(jnp.logical_not(has_high))
    def _():
        yhalo[1] = jnp.zeros((3, 2, edge, depth), f32)

    for side in range(2):
        for c in range(3):
            put_lhs((6 + side * 3 + c) * ny, vhalo[side, c])
        put_lhs(12 * ny + side * 6 * edge, yhalo[side].reshape(6 * edge, depth))

    def spread_halo(step, carry):
        at = pl.ds(pl.multiple_of(step * wide, 128), wide)
        fine = jnp.dot(lhs[6 * ny : 12 * ny + 12 * edge, :], tbv[:, at], preferred_element_type=f32)
        velx[:, 0, body, at] = fine[0 : 3 * ny].reshape(3, ny, wide)
        velx[:, 3, body, at] = fine[3 * ny : 6 * ny].reshape(3, ny, wide)
        low = fine[6 * ny : 6 * ny + 6 * edge].reshape(3, 2, edge, wide)
        high = fine[6 * ny + 6 * edge :].reshape(3, 2, edge, wide)
        velx[:, 1:3, 0:edge, at] = low
        velx[:, 1:3, edge + ny :, at] = high
        return carry

    lax.fori_loop(0, 3, spread_halo, 0)

    quarter = time_step

    def update_rows(step, carry):
        plane = step // (ny // 8)
        first = pl.multiple_of(edge + (step % (ny // 8)) * 8, 8)
        here = pl.ds(first, 8)
        around = pl.ds(pl.multiple_of(first - 8, 8), 24)
        target = pl.ds(pl.multiple_of(first - edge, 8), 8)
        speed = [quarter * velx[a, plane + 1, here, :] for a in range(3)]
        plus = [jnp.maximum(s, 0.0) for s in speed]
        minus = [jnp.maximum(-s, 0.0) for s in speed]
        drain = (jnp.abs(speed[0]) + jnp.abs(speed[1])) + jnp.abs(speed[2])
        keep = (1.0 - drain) - (time_step / relax_time) * fac[plane + 1, here, :]
        centre = [confx[c, plane + 1, here, :] for c in range(6)]
        grown = []
        for a in range(3):
            tall = velx[a, plane + 1, around, :]
            grad = (
                (0.5 * quarter) * (velx[a, plane + 2, here, :] - velx[a, plane, here, :]),
                (0.5 * quarter) * (tall[9:17] - tall[7:15]),
                quarter * veldz[a, plane, target, :],
            )
            grown.append(
                [
                    (grad[0] * centre[component_index[0][b]] + grad[1] * centre[component_index[1][b]])
                    + grad[2] * centre[component_index[2][b]]
                    for b in range(3)
                ]
            )
        for c, (a, b) in enumerate(((0, 0), (0, 1), (0, 2), (1, 1), (1, 2), (2, 2))):
            tall = confx[c, plane + 1, around, :]
            total = grown[a][b] + grown[b][a]
            total = total + keep * centre[c]
            total = total + plus[0] * confx[c, plane, here, :]
            total = total + minus[0] * confx[c, plane + 2, here, :]
            total = total + plus[1] * tall[7:15]
            total = total + minus[1] * tall[9:17]
            total = total + plus[2] * pltpu.roll(centre[c], 1, 1)
            total = total + minus[2] * pltpu.roll(centre[c], nz - 1, 1)
            if a == b:
                total = total + time_step / relax_time
            nxt[c, plane, target, :] = total
        return carry

    lax.fori_loop(0, 2 * (ny // 8), update_rows, 0)
    store_out = pltpu.make_async_copy(nxt, out, out_sem.at[0])
    store_out.start()

    exchange_recv(osend, orecv, o2a_send, o2a_recv, own_sem.at[1])

    def unpack(cm, carry):
        pair = orecv[:, cm, :]
        sbuf[cm, pl.ds(0, ngz, stride=2), :] = pair[:, 0:ny]
        sbuf[cm, pl.ds(1, ngz, stride=2), :] = pair[:, ny : 2 * ny]
        return carry

    lax.fori_loop(0, 3 * nm, unpack, 0)
    store_stress = pltpu.make_async_copy(sbuf, sout, out_sem.at[1])
    store_stress.start()

    exchange_sent(send, recv, a2a_send, a2a_recv)
    exchange_sent(osend, orecv, o2a_send, o2a_recv)
    for c in range(6):
        cx_up[c].wait_send()
        cx_down[c].wait_send()
    vx_up.wait_send()
    vx_down.wait_send()

    @pl.when(has_high)
    def _():
        cy_up.wait_send()
        vy_up.wait_send()

    @pl.when(has_low)
    def _():
        cy_down.wait_send()
        vy_down.wait_send()

    store_out.wait()
    store_stress.wait()


def shards(velocity_modes, conformation):
    ngy = lax.axis_size("gy")
    ngz = lax.axis_size("gz")
    _, planes, ny, nm = velocity_modes.shape
    nz = conformation.shape[3]
    modes = nm * ngz
    depth = round_up(modes, 128)
    tab_b, tab_s = (jnp.asarray(t) for t in spanwise_tables(modes, nz, depth))
    vm = jnp.transpose(velocity_modes, (0, 3, 1, 2)).reshape(3 * nm, planes, ny)
    f32, bf16 = jnp.float32, jnp.bfloat16
    dma = pltpu.SemaphoreType.DMA
    anywhere = pl.BlockSpec(memory_space=pl.ANY)
    out, sout = pl.pallas_call(
        functools.partial(kernel, (ngy, ngz, nm, ny, nz, depth)),
        name="fene_step",
        out_shape=(
            jax.ShapeDtypeStruct(conformation.shape, f32),
            jax.ShapeDtypeStruct(vm.shape, f32),
        ),
        in_specs=[anywhere] * 4,
        out_specs=[anywhere] * 2,
        scratch_shapes=[
            pltpu.VMEM((3 * nm, planes, ny), f32),
            pltpu.VMEM((6, 4, ny + 2 * edge, nz), f32),
            pltpu.VMEM((4, ny + 2 * edge, nz), f32),
            pltpu.VMEM((ngz, 3 * nm, 2 * ny), f32),
            pltpu.VMEM((ngz, 3 * nm, 2 * ny), f32),
            pltpu.VMEM((ngz, 3 * nm, 2 * ny), f32),
            pltpu.VMEM((ngz, 3 * nm, 2 * ny), f32),
            pltpu.VMEM((3, depth, 2 * ny), f32),
            pltpu.VMEM((3, 2, ny, depth), f32),
            pltpu.VMEM((2, 3, ny, depth), f32),
            pltpu.VMEM((2, 3, 2, edge, depth), f32),
            pltpu.VMEM((12 * ny + 12 * edge, 3 * depth), bf16),
            pltpu.VMEM((3, 4, ny + 2 * edge, nz), f32),
            pltpu.VMEM((3, 2, ny, nz), f32),
            pltpu.VMEM((6, 2, ny, nz), f32),
            pltpu.VMEM((3 * depth, nz), bf16),
            pltpu.VMEM((3 * depth, nz), bf16),
            pltpu.VMEM((4, 6 * ny, nz), bf16),
            pltpu.VMEM((modes, 6 * ny), f32),
            pltpu.VMEM((3 * nm, planes, ny), f32),
            dma((2,)), dma((4,)), dma((2,)), dma((2,)),
            dma((ngz,)), dma((ngz,)), dma((ngz,)), dma((ngz,)),
            dma((2, 6)), dma((2, 6)), dma((2,)), dma((2,)),
            dma((2,)), dma((2,)), dma((2,)), dma((2,)),
        ],
        compiler_params=pltpu.CompilerParams(
            collective_id=0, has_side_effects=True, vmem_limit_bytes=60 << 20
        ),
    )(vm, conformation, tab_b, tab_s)
    stress = jnp.transpose(sout.reshape(3, nm, planes, ny), (0, 2, 3, 1))
    return out, stress


def solution(mesh):
    return jax.shard_map(
        shards,
        mesh=mesh,
        in_specs=(P(None, None, "gy", "gz"), P(None, "gz", "gy", None)),
        out_specs=(P(None, "gz", "gy", None), P(None, None, "gy", "gz")),
        check_vma=False,
    )
```

```python
import functools
import math

import jax
import jax.numpy as jnp
import ml_dtypes
import numpy as np
from jax import lax
from jax.experimental import pallas as pl
from jax.experimental.pallas import tpu as pltpu
from jax.sharding import PartitionSpec as P

max_extension = 60.0
time_step = 0.25
relax_time = 4.0
stress_scale = 0.2
component_index = ((0, 1, 2), (1, 3, 4), (2, 4, 5))
MESH = pl.DeviceIdType.MESH
edge = 8


def round_up(value, unit):
    return (value + unit - 1) // unit * unit


@functools.lru_cache
def spanwise_tables(modes, points, depth):
    half = modes // 2
    index_j = np.arange(modes, dtype=np.int64)
    index_n = np.arange(points, dtype=np.int64)
    wave = np.where(index_j < half, index_j, index_j - half + 1)
    theta = (wave[:, None] * index_n[None, :] % points) * (2.0 * math.pi / points)
    rate = wave[:, None] * (2.0 * math.pi / points)
    is_cosine = (index_j < half)[:, None]
    basis = np.where(is_cosine, np.cos(theta), np.sin(theta))
    slope = np.where(is_cosine, -rate * np.sin(theta), rate * np.cos(theta))
    tables = []
    for table in (basis, slope):
        table = np.pad(table, ((0, depth - modes), (0, 0))).astype(np.float32)
        head = table.astype(ml_dtypes.bfloat16)
        rest = (table - head.astype(np.float32)).astype(ml_dtypes.bfloat16)
        tables.append(np.concatenate([head, rest], axis=0))
    return tables


def split(value):
    head = value.astype(jnp.bfloat16)
    return head, (value - head.astype(jnp.float32)).astype(jnp.bfloat16)


def kernel(
    dims,
    vm, conf, tab_b, tab_s,
    out, sout,
    vmv, confx, fac, send, recv, osend, orecv, cols, rows, vhalo, yhalo, lhs, velx, veldz,
    nxt, tbv, tsv, pull, res, sbuf,
    load_sem, tab_sem, own_sem, out_sem,
    a2a_send, a2a_recv, o2a_send, o2a_recv,
    cx_send, cx_recv, cy_send, cy_recv, vx_send, vx_recv, vy_send, vy_recv,
):
    ngy, ngz, nm, ny, nz, depth = dims
    modes = nm * ngz
    gy = lax.axis_index("gy")
    gz = lax.axis_index("gz")
    right = lax.rem(gz + 1, ngz)
    left = lax.rem(gz + ngz - 1, ngz)
    has_low = gy > 0
    has_high = gy < ngy - 1
    body = slice(edge, edge + ny)
    tall = send.shape[0] // ngz
    f32 = jnp.float32
    pieces = ((0, 2 * nz // 3), (2 * nz // 3, nz // 3))

    load_vm = pltpu.make_async_copy(vm, vmv, load_sem.at[0])
    load_vm.start()
    load_conf = pltpu.make_async_copy(conf, confx.at[:, 1:3, body, :], load_sem.at[1])
    load_conf.start()
    table_loads = []
    for index, (source, target) in enumerate(((tab_b, tbv), (tab_s, tsv))):
        table_loads.append(
            pltpu.make_async_copy(source, target.at[0 : 2 * depth], tab_sem.at[2 * index])
        )
        table_loads.append(
            pltpu.make_async_copy(
                source.at[0:depth], target.at[2 * depth : 3 * depth], tab_sem.at[2 * index + 1]
            )
        )
    for load in table_loads:
        load.start()

    ring = ngz // 4
    core = lax.rem(gz, 2)
    chip = lax.rem(lax.div(gz, 2), ring)
    high = lax.div(gz, 2 * ring)

    def peer_of(step, way):
        turn = lax.div(step, 4)
        hop = lax.div(turn + 1, 2) * (2 * lax.rem(turn, 2) - 1)
        return (
            lax.rem(high + lax.rem(lax.div(step, 2), 2), 2) * (2 * ring)
            + lax.rem(chip + way * hop + ring, ring) * 2
            + lax.rem(core + lax.rem(step, 2), 2)
        )

    barrier = pltpu.get_barrier_semaphore()

    def greet(step, carry):
        peer = lax.rem(gz + step, ngz)
        pl.semaphore_signal(barrier, inc=1, device_id=(gy, peer), device_id_type=MESH)
        return carry

    lax.fori_loop(1, ngz, greet, 0)

    @pl.when(has_low)
    def _():
        pl.semaphore_signal(barrier, inc=1, device_id=(gy - 1, gz), device_id_type=MESH)

    @pl.when(has_high)
    def _():
        pl.semaphore_signal(barrier, inc=1, device_id=(gy + 1, gz), device_id_type=MESH)

    load_vm.wait()

    def pack(cm, carry):
        even = vmv[cm, pl.ds(0, ngz, stride=2), :]
        odd = vmv[cm, pl.ds(1, ngz, stride=2), :]
        send[pl.ds(cm, ngz, stride=tall), :] = jnp.concatenate([even, odd], axis=1)
        return carry

    lax.fori_loop(0, 3 * nm, pack, 0, unroll=2)

    low_count = lax.div(gy + ngy - 1, ngy)
    high_count = lax.div(2 * ngy - 2 - gy, ngy)
    pl.semaphore_wait(barrier, ngz - 1 + low_count + high_count)

    cx_up = [
        pltpu.make_async_remote_copy(
            conf.at[c, 1], confx.at[c, 0, body, :], cx_send.at[0, c], cx_recv.at[0, c],
            device_id=(gy, right), device_id_type=MESH,
        )
        for c in range(6)
    ]
    cx_down = [
        pltpu.make_async_remote_copy(
            conf.at[c, 0], confx.at[c, 3, body, :], cx_send.at[1, c], cx_recv.at[1, c],
            device_id=(gy, left), device_id_type=MESH,
        )
        for c in range(6)
    ]
    cy_up = pltpu.make_async_remote_copy(
        conf.at[:, :, ny - edge : ny, :], confx.at[:, 1:3, 0:edge, :],
        cy_send.at[0], cy_recv.at[0], device_id=(gy + 1, gz), device_id_type=MESH,
    )
    cy_down = pltpu.make_async_remote_copy(
        conf.at[:, :, 0:edge, :], confx.at[:, 1:3, edge + ny : ny + 2 * edge, :],
        cy_send.at[1], cy_recv.at[1], device_id=(gy - 1, gz), device_id_type=MESH,
    )
    def words(source, peer):
        return source.at[pl.ds(pl.multiple_of(peer * tall, 8), 3 * nm), :]

    def message(source, target, send_sem, recv_sem, mine, theirs, peer):
        return pltpu.make_async_remote_copy(
            words(source, mine), target.at[theirs], send_sem.at[mine], recv_sem.at[theirs],
            device_id=(gy, peer), device_id_type=MESH,
        )

    def exchange_start(source, target, send_sem, recv_sem, own):
        def start(step, carry):
            peer = peer_of(step, 1)
            message(source, target, send_sem, recv_sem, peer, gz, peer).start()
            return carry

        lax.fori_loop(1, ngz, start, 0)
        pltpu.make_async_copy(words(source, gz), target.at[gz], own).start()

    def exchange_recv(source, target, send_sem, recv_sem, own, use):
        pltpu.make_async_copy(words(source, gz), target.at[gz], own).wait()
        use(gz)

        def wait(step, carry):
            peer = peer_of(step, -1)
            message(source, target, send_sem, recv_sem, peer, peer, peer).wait_recv()
            use(peer)
            return carry

        lax.fori_loop(1, ngz, wait, 0)

    def exchange_sent(source, target, send_sem, recv_sem):
        def wait(step, carry):
            peer = peer_of(step, 1)
            message(source, target, send_sem, recv_sem, peer, peer, peer).wait_send()
            return carry

        lax.fori_loop(1, ngz, wait, 0)

    exchange_start(send, recv, a2a_send, a2a_recv, own_sem.at[0])
    for c in range(6):
        cx_up[c].start()
        cx_down[c].start()

    @pl.when(has_high)
    def _():
        cy_up.start()

    @pl.when(has_low)
    def _():
        cy_down.start()

    load_conf.wait()
    for load in table_loads:
        load.wait()

    @pl.when(has_low)
    def _():
        cy_up.wait_recv()

    @pl.when(has_high)
    def _():
        cy_down.wait_recv()

    @pl.when(jnp.logical_not(has_low))
    def _():
        confx[:, 1:3, 0:edge, :] = jnp.zeros((6, 2, edge, nz), f32)

    @pl.when(jnp.logical_not(has_high))
    def _():
        confx[:, 1:3, edge + ny : ny + 2 * edge, :] = jnp.zeros((6, 2, edge, nz), f32)

    def factor_of(plane, at):
        trace = confx[0, plane, at, :] + confx[3, plane, at, :] + confx[5, plane, at, :]
        return (max_extension - 3.0) / (max_extension - trace)

    def factor_rows(block, carry):
        at = pl.ds(pl.multiple_of(block * 8, 8), 8)
        fac[0, at, :] = factor_of(1, at)
        fac[1, at, :] = factor_of(2, at)
        return carry

    lax.fori_loop(0, ny // 8 + 2, factor_rows, 0)

    weight = 2.0 / nz

    def own_rows(step, carry):
        first = pl.multiple_of(edge + step * 16, 8)
        here = pl.ds(first, 16)
        around = pl.ds(pl.multiple_of(first - 8, 8), 32)
        target = pl.ds(pl.multiple_of(step * 16, 16), 16)
        for plane in range(2):
            for row in range(3):
                cx, cy, cz = component_index[row]
                pulled = fac[plane, around, :] * confx[cy, plane + 1, around, :]
                other = fac[1 - plane, here, :] * confx[cx, 2 - plane, here, :]
                along = pulled[9:25] - pulled[7:23]
                nxt[row, plane, target, :] = along + other if plane == 0 else along - other
                spanwise = fac[plane, here, :] * confx[cz, plane + 1, here, :]
                at = pl.ds(pl.multiple_of((row * 2 + plane) * ny + step * 16, 16), 16)
                head, rest = split(spanwise * (-stress_scale * weight))
                pull[2, at, :] = head
                pull[3, at, :] = rest
        return carry

    lax.fori_loop(0, ny // 16, own_rows, 0)

    chunk = modes // 2

    def across(a, b):
        return lax.dot_general(a, b, (((1,), (1,)), ((), ())), preferred_element_type=f32)

    def project(table, which, step):
        first = pl.multiple_of(step * chunk, 16)
        head = table[pl.ds(first, chunk), :]
        rest = table[pl.ds(pl.multiple_of(depth + first, 16), chunk), :]
        total = across(head, pull[which]) + across(head, pull[which + 1])
        return total + across(rest, pull[which]), pl.ds(first, chunk)

    def project_spanwise(step, carry):
        total, at = project(tsv, 2, step)
        res[at, :] = total
        return carry

    lax.fori_loop(0, 2, project_spanwise, 0)

    for c in range(3):
        cols[c, modes:depth, :] = jnp.zeros((depth - modes, 2 * ny), f32)

    def place(k):
        for c in range(3):
            cols[c, pl.ds(k * nm, nm), :] = recv[k, c * nm : (c + 1) * nm, :]

    exchange_recv(send, recv, a2a_send, a2a_recv, own_sem.at[0], place)
    for c in range(3):
        turned = cols[c].T
        rows[c] = turned.reshape(2, ny, depth)

    vx_up = pltpu.make_async_remote_copy(
        rows.at[:, 1], vhalo.at[0], vx_send.at[0], vx_recv.at[0],
        device_id=(gy, right), device_id_type=MESH,
    )
    vx_down = pltpu.make_async_remote_copy(
        rows.at[:, 0], vhalo.at[1], vx_send.at[1], vx_recv.at[1],
        device_id=(gy, left), device_id_type=MESH,
    )
    vy_up = pltpu.make_async_remote_copy(
        rows.at[:, :, ny - edge : ny, :], yhalo.at[0], vy_send.at[0], vy_recv.at[0],
        device_id=(gy + 1, gz), device_id_type=MESH,
    )
    vy_down = pltpu.make_async_remote_copy(
        rows.at[:, :, 0:edge, :], yhalo.at[1], vy_send.at[1], vy_recv.at[1],
        device_id=(gy - 1, gz), device_id_type=MESH,
    )
    vx_up.start()
    vx_down.start()

    @pl.when(has_high)
    def _():
        vy_up.start()

    @pl.when(has_low)
    def _():
        vy_down.start()

    def put_lhs(first, value):
        head, rest = split(value)
        at = slice(first, first + value.shape[0])
        lhs[at, 0:depth] = head
        lhs[at, depth : 2 * depth] = head
        lhs[at, 2 * depth : 3 * depth] = rest

    for c in range(3):
        for p in range(2):
            put_lhs((c * 2 + p) * ny, rows[c, p])

    for c in range(6):
        cx_up[c].wait_recv()
        cx_down[c].wait_recv()

    def halo_rows(step, carry):
        here = pl.ds(pl.multiple_of(edge + step * 16, 8), 16)
        target = pl.ds(pl.multiple_of(step * 16, 16), 16)
        for plane in range(2):
            outer = factor_of(3 * plane, here)
            for row in range(3):
                pulled = outer * confx[component_index[row][0], 3 * plane, here, :]
                along = nxt[row, plane, target, :]
                along = along - pulled if plane == 0 else along + pulled
                at = pl.ds(pl.multiple_of((row * 2 + plane) * ny + step * 16, 16), 16)
                head, rest = split(along * (0.5 * stress_scale * weight))
                pull[0, at, :] = head
                pull[1, at, :] = rest
        return carry

    lax.fori_loop(0, ny // 16, halo_rows, 0)

    def project_along(step, carry):
        total, at = project(tbv, 0, step)
        res[at, :] = res[at, :] + total
        return carry

    lax.fori_loop(0, 2, project_along, 0)
    head_row = lax.broadcasted_iota(jnp.int32, (8, 6 * ny), 0) == 0
    res[0:8, :] = jnp.where(head_row, 0.5 * res[0:8, :], res[0:8, :])
    for k in range(ngz):
        for c in range(3):
            osend[k * tall + c * nm : k * tall + (c + 1) * nm, :] = res[
                k * nm : (k + 1) * nm, c * 2 * ny : (c + 1) * 2 * ny
            ]
    exchange_start(osend, orecv, o2a_send, o2a_recv, own_sem.at[1])

    for first, wide in pieces:
        at = slice(first, first + wide)
        fine = jnp.dot(lhs[0 : 6 * ny, :], tbv[:, at], preferred_element_type=f32)
        velx[:, 1:3, body, at] = fine.reshape(3, 2, ny, wide)
        fine = jnp.dot(lhs[0 : 6 * ny, :], tsv[:, at], preferred_element_type=f32)
        veldz[:, :, :, at] = fine.reshape(3, 2, ny, wide)

    vx_up.wait_recv()
    vx_down.wait_recv()

    @pl.when(has_low)
    def _():
        vy_up.wait_recv()

    @pl.when(has_high)
    def _():
        vy_down.wait_recv()

    @pl.when(jnp.logical_not(has_low))
    def _():
        yhalo[0] = jnp.zeros((3, 2, edge, depth), f32)

    @pl.when(jnp.logical_not(has_high))
    def _():
        yhalo[1] = jnp.zeros((3, 2, edge, depth), f32)

    for side in range(2):
        for c in range(3):
            put_lhs((6 + side * 3 + c) * ny, vhalo[side, c])
        put_lhs(12 * ny + side * 6 * edge, yhalo[side].reshape(6 * edge, depth))

    for first, wide in pieces:
        at = slice(first, first + wide)
        fine = jnp.dot(lhs[6 * ny : 12 * ny + 12 * edge, :], tbv[:, at], preferred_element_type=f32)
        velx[:, 0, body, at] = fine[0 : 3 * ny].reshape(3, ny, wide)
        velx[:, 3, body, at] = fine[3 * ny : 6 * ny].reshape(3, ny, wide)
        low = fine[6 * ny : 6 * ny + 6 * edge].reshape(3, 2, edge, wide)
        velx[:, 1:3, 0:edge, at] = low
        velx[:, 1:3, edge + ny :, at] = fine[6 * ny + 6 * edge :].reshape(3, 2, edge, wide)

    quarter = time_step

    def update_rows(step, carry):
        plane = step // (ny // 8)
        first = pl.multiple_of(edge + (step % (ny // 8)) * 8, 8)
        here = pl.ds(first, 8)
        around = pl.ds(pl.multiple_of(first - 8, 8), 24)
        target = pl.ds(pl.multiple_of(first - edge, 8), 8)
        speed = [quarter * velx[a, plane + 1, here, :] for a in range(3)]
        plus = [jnp.maximum(s, 0.0) for s in speed]
        minus = [jnp.maximum(-s, 0.0) for s in speed]
        drain = (jnp.abs(speed[0]) + jnp.abs(speed[1])) + jnp.abs(speed[2])
        keep = (1.0 - drain) - (time_step / relax_time) * fac[plane, here, :]
        centre = [confx[c, plane + 1, here, :] for c in range(6)]
        grown = []
        for a in range(3):
            tall = velx[a, plane + 1, around, :]
            grad = (
                (0.5 * quarter) * (velx[a, plane + 2, here, :] - velx[a, plane, here, :]),
                (0.5 * quarter) * (tall[9:17] - tall[7:15]),
                quarter * veldz[a, plane, target, :],
            )
            grown.append(
                [
                    (grad[0] * centre[component_index[0][b]] + grad[1] * centre[component_index[1][b]])
                    + grad[2] * centre[component_index[2][b]]
                    for b in range(3)
                ]
            )
        for c, (a, b) in enumerate(((0, 0), (0, 1), (0, 2), (1, 1), (1, 2), (2, 2))):
            tall = confx[c, plane + 1, around, :]
            total = grown[a][b] + grown[b][a]
            total = total + keep * centre[c]
            total = total + plus[0] * confx[c, plane, here, :]
            total = total + minus[0] * confx[c, plane + 2, here, :]
            total = total + plus[1] * tall[7:15]
            total = total + minus[1] * tall[9:17]
            total = total + plus[2] * pltpu.roll(centre[c], 1, 1)
            total = total + minus[2] * pltpu.roll(centre[c], nz - 1, 1)
            if a == b:
                total = total + time_step / relax_time
            nxt[c, plane, target, :] = total
        return carry

    lax.fori_loop(0, 2 * (ny // 8), update_rows, 0)
    store_out = pltpu.make_async_copy(nxt, out, out_sem.at[0])
    store_out.start()

    def unpack(k):
        pair = orecv[k]
        sbuf[pl.ds(2 * k, 3 * nm, stride=2 * ngz), :] = pair[:, 0:ny]
        sbuf[pl.ds(2 * k + 1, 3 * nm, stride=2 * ngz), :] = pair[:, ny : 2 * ny]

    exchange_recv(osend, orecv, o2a_send, o2a_recv, own_sem.at[1], unpack)
    store_stress = pltpu.make_async_copy(sbuf, sout, out_sem.at[1])
    store_stress.start()

    exchange_sent(send, recv, a2a_send, a2a_recv)
    exchange_sent(osend, orecv, o2a_send, o2a_recv)
    for c in range(6):
        cx_up[c].wait_send()
        cx_down[c].wait_send()
    vx_up.wait_send()
    vx_down.wait_send()

    @pl.when(has_high)
    def _():
        cy_up.wait_send()
        vy_up.wait_send()

    @pl.when(has_low)
    def _():
        cy_down.wait_send()
        vy_down.wait_send()

    store_out.wait()
    store_stress.wait()


def shards(velocity_modes, conformation):
    ngy = lax.axis_size("gy")
    ngz = lax.axis_size("gz")
    _, planes, ny, nm = velocity_modes.shape
    nz = conformation.shape[3]
    modes = nm * ngz
    depth = round_up(modes, 128)
    tab_b, tab_s = (jnp.asarray(t) for t in spanwise_tables(modes, nz, depth))
    vm = jnp.transpose(velocity_modes, (0, 3, 1, 2)).reshape(3 * nm, planes, ny)
    f32, bf16 = jnp.float32, jnp.bfloat16
    dma = pltpu.SemaphoreType.DMA
    anywhere = pl.BlockSpec(memory_space=pl.ANY)
    out, sout = pl.pallas_call(
        functools.partial(kernel, (ngy, ngz, nm, ny, nz, depth)),
        name="fene_step",
        out_shape=(
            jax.ShapeDtypeStruct(conformation.shape, f32),
            jax.ShapeDtypeStruct((3 * nm * planes, ny), f32),
        ),
        in_specs=[anywhere] * 4,
        out_specs=[anywhere] * 2,
        scratch_shapes=[
            pltpu.VMEM((3 * nm, planes, ny), f32),
            pltpu.VMEM((6, 4, ny + 2 * edge, nz), f32),
            pltpu.VMEM((2, ny + 2 * edge, nz), f32),
            pltpu.VMEM((ngz * round_up(3 * nm, 8), 2 * ny), f32),
            pltpu.VMEM((ngz, 3 * nm, 2 * ny), f32),
            pltpu.VMEM((ngz * round_up(3 * nm, 8), 2 * ny), f32),
            pltpu.VMEM((ngz, 3 * nm, 2 * ny), f32),
            pltpu.VMEM((3, depth, 2 * ny), f32),
            pltpu.VMEM((3, 2, ny, depth), f32),
            pltpu.VMEM((2, 3, ny, depth), f32),
            pltpu.VMEM((2, 3, 2, edge, depth), f32),
            pltpu.VMEM((12 * ny + 12 * edge, 3 * depth), bf16),
            pltpu.VMEM((3, 4, ny + 2 * edge, nz), f32),
            pltpu.VMEM((3, 2, ny, nz), f32),
            pltpu.VMEM((6, 2, ny, nz), f32),
            pltpu.VMEM((3 * depth, nz), bf16),
            pltpu.VMEM((3 * depth, nz), bf16),
            pltpu.VMEM((4, 6 * ny, nz), bf16),
            pltpu.VMEM((modes, 6 * ny), f32),
            pltpu.VMEM((3 * nm * planes, ny), f32),
            dma((2,)), dma((4,)), dma((2,)), dma((2,)),
            dma((ngz,)), dma((ngz,)), dma((ngz,)), dma((ngz,)),
            dma((2, 6)), dma((2, 6)), dma((2,)), dma((2,)),
            dma((2,)), dma((2,)), dma((2,)), dma((2,)),
        ],
        compiler_params=pltpu.CompilerParams(
            collective_id=0, has_side_effects=True, vmem_limit_bytes=60 << 20
        ),
    )(vm, conformation, tab_b, tab_s)
    stress = jnp.transpose(sout.reshape(3, nm, planes, ny), (0, 2, 3, 1))
    return out, stress


def solution(mesh):
    return jax.shard_map(
        shards,
        mesh=mesh,
        in_specs=(P(None, None, "gy", "gz"), P(None, "gz", "gy", None)),
        out_specs=(P(None, "gz", "gy", None), P(None, None, "gy", "gz")),
        check_vma=False,
    )
```

```python
import functools
import math

import jax
import jax.numpy as jnp
import ml_dtypes
import numpy as np
from jax import lax
from jax.experimental import pallas as pl
from jax.experimental.pallas import tpu as pltpu
from jax.sharding import PartitionSpec as P

max_extension = 60.0
time_step = 0.25
relax_time = 4.0
stress_scale = 0.2
component_index = ((0, 1, 2), (1, 3, 4), (2, 4, 5))
MESH = pl.DeviceIdType.MESH
edge = 8


def round_up(value, unit):
    return (value + unit - 1) // unit * unit


@functools.lru_cache
def spanwise_tables(modes, points, depth):
    half = modes // 2
    index_j = np.arange(modes, dtype=np.int64)
    index_n = np.arange(points, dtype=np.int64)
    wave = np.where(index_j < half, index_j, index_j - half + 1)
    theta = (wave[:, None] * index_n[None, :] % points) * (2.0 * math.pi / points)
    rate = wave[:, None] * (2.0 * math.pi / points)
    is_cosine = (index_j < half)[:, None]
    basis = np.where(is_cosine, np.cos(theta), np.sin(theta))
    slope = np.where(is_cosine, -rate * np.sin(theta), rate * np.cos(theta))
    tables = []
    for table in (basis, slope):
        table = np.pad(table, ((0, depth - modes), (0, 0))).astype(np.float32)
        head = table.astype(ml_dtypes.bfloat16)
        rest = (table - head.astype(np.float32)).astype(ml_dtypes.bfloat16)
        tables.append(np.concatenate([head, rest], axis=0))
    return tables


def split(value):
    head = value.astype(jnp.bfloat16)
    return head, (value - head.astype(jnp.float32)).astype(jnp.bfloat16)


def kernel(
    dims,
    vm, conf, tab_b, tab_s,
    nxt, sbuf,
    vmv, confx, fac, send, recv, osend, orecv, cols, rows, vhalo, yhalo, vedge, cedge, cnear, lhs, velx, veldz,
    tbv, tsv, pull, res,
    load_sem, tab_sem, own_sem,
    a2a_send, a2a_recv, o2a_send, o2a_recv,
    cx_send, cx_recv, cy_send, cy_recv, vx_send, vx_recv, vy_send, vy_recv,
):
    ngy, ngz, nm, ny, nz, depth = dims
    modes = nm * ngz
    gy = lax.axis_index("gy")
    gz = lax.axis_index("gz")
    right = lax.rem(gz + 1, ngz)
    left = lax.rem(gz + ngz - 1, ngz)
    has_low = gy > 0
    has_high = gy < ngy - 1
    body = slice(edge, edge + ny)
    tall = send.shape[0] // ngz
    f32 = jnp.float32
    pieces = ((0, 2 * nz // 3), (2 * nz // 3, nz // 3))

    load_vm = pltpu.make_async_copy(vm, vmv, load_sem.at[0])
    load_vm.start()
    load_conf = pltpu.make_async_copy(conf, confx.at[:, 1:3, body, :], load_sem.at[1])
    load_conf.start()
    table_loads = []
    for index, (source, target) in enumerate(((tab_b, tbv), (tab_s, tsv))):
        table_loads.append(
            pltpu.make_async_copy(source, target.at[0 : 2 * depth], tab_sem.at[2 * index])
        )
        table_loads.append(
            pltpu.make_async_copy(
                source.at[0:depth], target.at[2 * depth : 3 * depth], tab_sem.at[2 * index + 1]
            )
        )
    for load in table_loads:
        load.start()

    ring = ngz // 4
    core = lax.rem(gz, 2)
    chip = lax.rem(lax.div(gz, 2), ring)
    high = lax.div(gz, 2 * ring)

    def peer_of(step, way):
        turn = lax.div(step, 4)
        hop = lax.div(turn + 1, 2) * (2 * lax.rem(turn, 2) - 1)
        return (
            lax.rem(high + lax.rem(lax.div(step, 2), 2), 2) * (2 * ring)
            + lax.rem(chip + way * hop + ring, ring) * 2
            + lax.rem(core + lax.rem(step, 2), 2)
        )

    barrier = pltpu.get_barrier_semaphore()

    def greet(step, carry):
        peer = lax.rem(gz + step, ngz)
        pl.semaphore_signal(barrier, inc=1, device_id=(gy, peer), device_id_type=MESH)
        return carry

    lax.fori_loop(1, ngz, greet, 0)

    @pl.when(has_low)
    def _():
        pl.semaphore_signal(barrier, inc=1, device_id=(gy - 1, gz), device_id_type=MESH)

    @pl.when(has_high)
    def _():
        pl.semaphore_signal(barrier, inc=1, device_id=(gy + 1, gz), device_id_type=MESH)

    load_vm.wait()

    def pack(cm, carry):
        even = vmv[cm, pl.ds(0, ngz, stride=2), :]
        odd = vmv[cm, pl.ds(1, ngz, stride=2), :]
        send[pl.ds(cm, ngz, stride=tall), :] = jnp.concatenate([even, odd], axis=1)
        return carry

    lax.fori_loop(0, 3 * nm, pack, 0, unroll=2)

    low_count = lax.div(gy + ngy - 1, ngy)
    high_count = lax.div(2 * ngy - 2 - gy, ngy)
    pl.semaphore_wait(barrier, ngz - 1 + low_count + high_count)

    cx_up = [
        pltpu.make_async_remote_copy(
            conf.at[c, 1], confx.at[c, 0, body, :], cx_send.at[0, c], cx_recv.at[0, c],
            device_id=(gy, right), device_id_type=MESH,
        )
        for c in range(6)
    ]
    cx_down = [
        pltpu.make_async_remote_copy(
            conf.at[c, 0], confx.at[c, 3, body, :], cx_send.at[1, c], cx_recv.at[1, c],
            device_id=(gy, left), device_id_type=MESH,
        )
        for c in range(6)
    ]
    cy_up = pltpu.make_async_remote_copy(
        cedge.at[1], cnear.at[0],
        cy_send.at[0], cy_recv.at[0], device_id=(gy + 1, gz), device_id_type=MESH,
    )
    cy_down = pltpu.make_async_remote_copy(
        cedge.at[0], cnear.at[1],
        cy_send.at[1], cy_recv.at[1], device_id=(gy - 1, gz), device_id_type=MESH,
    )
    def words(source, peer):
        return source.at[pl.ds(pl.multiple_of(peer * tall, 8), 3 * nm), :]

    def message(source, target, send_sem, recv_sem, mine, theirs, peer):
        return pltpu.make_async_remote_copy(
            words(source, mine), target.at[theirs], send_sem.at[mine], recv_sem.at[theirs],
            device_id=(gy, peer), device_id_type=MESH,
        )

    def exchange_start(source, target, send_sem, recv_sem, own):
        def start(step, carry):
            peer = peer_of(step, 1)
            message(source, target, send_sem, recv_sem, peer, gz, peer).start()
            return carry

        lax.fori_loop(1, ngz, start, 0)
        pltpu.make_async_copy(words(source, gz), target.at[gz], own).start()

    def exchange_recv(source, target, send_sem, recv_sem, own, use):
        pltpu.make_async_copy(words(source, gz), target.at[gz], own).wait()
        use(gz)

        def wait(step, carry):
            peer = peer_of(step, -1)
            message(source, target, send_sem, recv_sem, peer, peer, peer).wait_recv()
            use(peer)
            return carry

        lax.fori_loop(1, ngz, wait, 0)

    def exchange_sent(source, target, send_sem, recv_sem):
        def wait(step, carry):
            peer = peer_of(step, 1)
            message(source, target, send_sem, recv_sem, peer, peer, peer).wait_send()
            return carry

        lax.fori_loop(1, ngz, wait, 0)

    exchange_start(send, recv, a2a_send, a2a_recv, own_sem.at[0])
    for c in (0, 3, 5, 1, 2):
        cx_up[c].start()
        cx_down[c].start()

    load_conf.wait()
    cedge[...] = jnp.zeros_like(cedge)
    for c in range(6):
        for p in range(2):
            at = slice(2 * c + p, 2 * c + p + 1)
            cedge[0, at, :] = confx[c, 1 + p, edge : edge + 1, :]
            cedge[1, at, :] = confx[c, 1 + p, edge + ny - 1 : edge + ny, :]

    @pl.when(has_high)
    def _():
        cy_up.start()

    @pl.when(has_low)
    def _():
        cy_down.start()

    for load in table_loads:
        load.wait()

    @pl.when(has_low)
    def _():
        cy_up.wait_recv()

    @pl.when(has_high)
    def _():
        cy_down.wait_recv()

    @pl.when(jnp.logical_not(has_low))
    def _():
        cnear[0] = jnp.zeros((16, nz), f32)

    @pl.when(jnp.logical_not(has_high))
    def _():
        cnear[1] = jnp.zeros((16, nz), f32)

    blank = jnp.zeros((edge - 1, nz), f32)
    for c in range(6):
        for p in range(2):
            at = slice(2 * c + p, 2 * c + p + 1)
            confx[c, 1 + p, 0:edge, :] = jnp.concatenate([blank, cnear[0, at, :]], axis=0)
            confx[c, 1 + p, edge + ny :, :] = jnp.concatenate([cnear[1, at, :], blank], axis=0)

    def factor_of(plane, at):
        trace = confx[0, plane, at, :] + confx[3, plane, at, :] + confx[5, plane, at, :]
        return (max_extension - 3.0) / (max_extension - trace)

    def factor_rows(block, carry):
        at = pl.ds(pl.multiple_of(block * 8, 8), 8)
        fac[0, at, :] = factor_of(1, at)
        fac[1, at, :] = factor_of(2, at)
        return carry

    lax.fori_loop(0, ny // 8 + 2, factor_rows, 0)

    weight = 2.0 / nz

    def own_rows(step, carry):
        first = pl.multiple_of(edge + step * 16, 8)
        here = pl.ds(first, 16)
        around = pl.ds(pl.multiple_of(first - 8, 8), 32)
        target = pl.ds(pl.multiple_of(step * 16, 16), 16)
        for plane in range(2):
            for row in range(3):
                cx, cy, cz = component_index[row]
                pulled = fac[plane, around, :] * confx[cy, plane + 1, around, :]
                other = fac[1 - plane, here, :] * confx[cx, 2 - plane, here, :]
                along = pulled[9:25] - pulled[7:23]
                nxt[row, plane, target, :] = along + other if plane == 0 else along - other
                spanwise = fac[plane, here, :] * confx[cz, plane + 1, here, :]
                at = pl.ds(pl.multiple_of((row * 2 + plane) * ny + step * 16, 16), 16)
                head, rest = split(spanwise * (-stress_scale * weight))
                pull[2, at, :] = head
                pull[3, at, :] = rest
        return carry

    lax.fori_loop(0, ny // 16, own_rows, 0)

    chunk = modes // 2

    def across(a, b):
        return lax.dot_general(a, b, (((1,), (1,)), ((), ())), preferred_element_type=f32)

    def project(table, which, step):
        first = pl.multiple_of(step * chunk, 16)
        head = table[pl.ds(first, chunk), :]
        rest = table[pl.ds(pl.multiple_of(depth + first, 16), chunk), :]
        total = across(head, pull[which]) + across(head, pull[which + 1])
        return total + across(rest, pull[which]), pl.ds(first, chunk)

    def project_spanwise(step, carry):
        total, at = project(tsv, 2, step)
        res[at, :] = total
        return carry

    lax.fori_loop(0, 2, project_spanwise, 0)

    for c in range(3):
        cols[c, modes:depth, :] = jnp.zeros((depth - modes, 2 * ny), f32)

    def place(k):
        for c in range(3):
            cols[c, pl.ds(k * nm, nm), :] = recv[k, c * nm : (c + 1) * nm, :]

    exchange_recv(send, recv, a2a_send, a2a_recv, own_sem.at[0], place)
    for c in range(3):
        turned = cols[c].T
        rows[c] = turned.reshape(2, ny, depth)

    vx_up = pltpu.make_async_remote_copy(
        rows.at[:, 1], vhalo.at[0], vx_send.at[0], vx_recv.at[0],
        device_id=(gy, right), device_id_type=MESH,
    )
    vx_down = pltpu.make_async_remote_copy(
        rows.at[:, 0], vhalo.at[1], vx_send.at[1], vx_recv.at[1],
        device_id=(gy, left), device_id_type=MESH,
    )
    vy_up = pltpu.make_async_remote_copy(
        vedge.at[1], yhalo.at[0], vy_send.at[0], vy_recv.at[0],
        device_id=(gy + 1, gz), device_id_type=MESH,
    )
    vy_down = pltpu.make_async_remote_copy(
        vedge.at[0], yhalo.at[1], vy_send.at[1], vy_recv.at[1],
        device_id=(gy - 1, gz), device_id_type=MESH,
    )
    vx_up.start()
    vx_down.start()
    cx_up[4].start()
    cx_down[4].start()

    vedge[...] = jnp.zeros_like(vedge)
    for c in range(3):
        for p in range(2):
            at = slice(2 * c + p, 2 * c + p + 1)
            vedge[0, at, :] = rows[c, p, 0:1, :]
            vedge[1, at, :] = rows[c, p, ny - 1 : ny, :]

    @pl.when(has_high)
    def _():
        vy_up.start()

    @pl.when(has_low)
    def _():
        vy_down.start()

    def put_lhs(first, value):
        head, rest = split(value)
        at = slice(first, first + value.shape[0])
        lhs[at, 0:depth] = head
        lhs[at, depth : 2 * depth] = head
        lhs[at, 2 * depth : 3 * depth] = rest

    for c in range(3):
        for p in range(2):
            put_lhs((c * 2 + p) * ny, rows[c, p])

    for c in (0, 3, 5, 1, 2):
        cx_up[c].wait_recv()
        cx_down[c].wait_recv()

    def halo_rows(step, carry):
        here = pl.ds(pl.multiple_of(edge + step * 16, 8), 16)
        target = pl.ds(pl.multiple_of(step * 16, 16), 16)
        for plane in range(2):
            outer = factor_of(3 * plane, here)
            for row in range(3):
                pulled = outer * confx[component_index[row][0], 3 * plane, here, :]
                along = nxt[row, plane, target, :]
                along = along - pulled if plane == 0 else along + pulled
                at = pl.ds(pl.multiple_of((row * 2 + plane) * ny + step * 16, 16), 16)
                head, rest = split(along * (0.5 * stress_scale * weight))
                pull[0, at, :] = head
                pull[1, at, :] = rest
        return carry

    lax.fori_loop(0, ny // 16, halo_rows, 0)

    def project_along(step, carry):
        total, at = project(tbv, 0, step)
        res[at, :] = res[at, :] + total
        return carry

    lax.fori_loop(0, 2, project_along, 0)
    head_row = lax.broadcasted_iota(jnp.int32, (8, 6 * ny), 0) == 0
    res[0:8, :] = jnp.where(head_row, 0.5 * res[0:8, :], res[0:8, :])
    for k in range(ngz):
        for c in range(3):
            osend[k * tall + c * nm : k * tall + (c + 1) * nm, :] = res[
                k * nm : (k + 1) * nm, c * 2 * ny : (c + 1) * 2 * ny
            ]
    exchange_start(osend, orecv, o2a_send, o2a_recv, own_sem.at[1])

    for first, wide in pieces:
        at = slice(first, first + wide)
        fine = jnp.dot(lhs[0 : 6 * ny, :], tbv[:, at], preferred_element_type=f32)
        velx[:, 1:3, body, at] = fine.reshape(3, 2, ny, wide)
        fine = jnp.dot(lhs[0 : 6 * ny, :], tsv[:, at], preferred_element_type=f32)
        veldz[:, :, :, at] = fine.reshape(3, 2, ny, wide)

    vx_up.wait_recv()
    vx_down.wait_recv()

    @pl.when(has_low)
    def _():
        vy_up.wait_recv()

    @pl.when(has_high)
    def _():
        vy_down.wait_recv()

    @pl.when(jnp.logical_not(has_low))
    def _():
        yhalo[0] = jnp.zeros((edge, depth), f32)

    @pl.when(jnp.logical_not(has_high))
    def _():
        yhalo[1] = jnp.zeros((edge, depth), f32)

    put_lhs(12 * ny, yhalo[...].reshape(2 * edge, depth))
    for side in range(2):
        for c in range(3):
            put_lhs((6 + side * 3 + c) * ny, vhalo[side, c])

    for first, wide in pieces:
        at = slice(first, first + wide)
        fine = jnp.dot(lhs[6 * ny : 12 * ny + 2 * edge, :], tbv[:, at], preferred_element_type=f32)
        velx[:, 0, body, at] = fine[0 : 3 * ny].reshape(3, ny, wide)
        velx[:, 3, body, at] = fine[3 * ny : 6 * ny].reshape(3, ny, wide)
        for c in range(3):
            for p in range(2):
                row = 6 * ny + 2 * c + p
                velx[c, 1 + p, edge - 1 : edge, at] = fine[row : row + 1]
                velx[c, 1 + p, edge + ny : edge + ny + 1, at] = fine[row + edge : row + edge + 1]

    quarter = time_step

    def update_rows(step, carry):
        plane = step // (ny // 8)
        first = pl.multiple_of(edge + (step % (ny // 8)) * 8, 8)
        here = pl.ds(first, 8)
        around = pl.ds(pl.multiple_of(first - 8, 8), 24)
        target = pl.ds(pl.multiple_of(first - edge, 8), 8)
        speed = [quarter * velx[a, plane + 1, here, :] for a in range(3)]
        plus = [jnp.maximum(s, 0.0) for s in speed]
        minus = [jnp.maximum(-s, 0.0) for s in speed]
        drain = (jnp.abs(speed[0]) + jnp.abs(speed[1])) + jnp.abs(speed[2])
        keep = (1.0 - drain) - (time_step / relax_time) * fac[plane, here, :]
        centre = [confx[c, plane + 1, here, :] for c in range(6)]
        grown = []
        for a in range(3):
            tall = velx[a, plane + 1, around, :]
            grad = (
                (0.5 * quarter) * (velx[a, plane + 2, here, :] - velx[a, plane, here, :]),
                (0.5 * quarter) * (tall[9:17] - tall[7:15]),
                quarter * veldz[a, plane, target, :],
            )
            grown.append(
                [
                    (grad[0] * centre[component_index[0][b]] + grad[1] * centre[component_index[1][b]])
                    + grad[2] * centre[component_index[2][b]]
                    for b in range(3)
                ]
            )
        for c, (a, b) in enumerate(((0, 0), (0, 1), (0, 2), (1, 1), (1, 2), (2, 2))):
            tall = confx[c, plane + 1, around, :]
            total = grown[a][b] + grown[b][a]
            total = total + keep * centre[c]
            total = total + plus[0] * confx[c, plane, here, :]
            total = total + minus[0] * confx[c, plane + 2, here, :]
            total = total + plus[1] * tall[7:15]
            total = total + minus[1] * tall[9:17]
            total = total + plus[2] * pltpu.roll(centre[c], 1, 1)
            total = total + minus[2] * pltpu.roll(centre[c], nz - 1, 1)
            if a == b:
                total = total + time_step / relax_time
            nxt[c, plane, target, :] = total
        return carry

    cx_up[4].wait_recv()
    cx_down[4].wait_recv()
    lax.fori_loop(0, 2 * (ny // 8), update_rows, 0)

    def unpack(k):
        pair = orecv[k]
        sbuf[pl.ds(2 * k, 3 * nm, stride=2 * ngz), :] = pair[:, 0:ny]
        sbuf[pl.ds(2 * k + 1, 3 * nm, stride=2 * ngz), :] = pair[:, ny : 2 * ny]

    exchange_recv(osend, orecv, o2a_send, o2a_recv, own_sem.at[1], unpack)

    exchange_sent(send, recv, a2a_send, a2a_recv)
    exchange_sent(osend, orecv, o2a_send, o2a_recv)
    for c in range(6):
        cx_up[c].wait_send()
        cx_down[c].wait_send()
    vx_up.wait_send()
    vx_down.wait_send()

    @pl.when(has_high)
    def _():
        cy_up.wait_send()
        vy_up.wait_send()

    @pl.when(has_low)
    def _():
        cy_down.wait_send()
        vy_down.wait_send()


def shards(velocity_modes, conformation):
    ngy = lax.axis_size("gy")
    ngz = lax.axis_size("gz")
    _, planes, ny, nm = velocity_modes.shape
    nz = conformation.shape[3]
    modes = nm * ngz
    depth = round_up(modes, 128)
    tab_b, tab_s = (jnp.asarray(t) for t in spanwise_tables(modes, nz, depth))
    vm = jnp.transpose(velocity_modes, (0, 3, 1, 2)).reshape(3 * nm, planes, ny)
    f32, bf16 = jnp.float32, jnp.bfloat16
    dma = pltpu.SemaphoreType.DMA
    anywhere = pl.BlockSpec(memory_space=pl.ANY)
    out, sout = pl.pallas_call(
        functools.partial(kernel, (ngy, ngz, nm, ny, nz, depth)),
        name="fene_step",
        out_shape=(
            pltpu.VMEM(conformation.shape, f32),
            pltpu.VMEM((3 * nm * planes, ny), f32),
        ),
        in_specs=[anywhere] * 4,
        out_specs=[pl.BlockSpec(memory_space=pltpu.VMEM)] * 2,
        scratch_shapes=[
            pltpu.VMEM((3 * nm, planes, ny), f32),
            pltpu.VMEM((6, 4, ny + 2 * edge, nz), f32),
            pltpu.VMEM((2, ny + 2 * edge, nz), f32),
            pltpu.VMEM((ngz * round_up(3 * nm, 8), 2 * ny), f32),
            pltpu.VMEM((ngz, 3 * nm, 2 * ny), f32),
            pltpu.VMEM((ngz * round_up(3 * nm, 8), 2 * ny), f32),
            pltpu.VMEM((ngz, 3 * nm, 2 * ny), f32),
            pltpu.VMEM((3, depth, 2 * ny), f32),
            pltpu.VMEM((3, 2, ny, depth), f32),
            pltpu.VMEM((2, 3, ny, depth), f32),
            pltpu.VMEM((2, edge, depth), f32),
            pltpu.VMEM((2, edge, depth), f32),
            pltpu.VMEM((2, 16, nz), f32),
            pltpu.VMEM((2, 16, nz), f32),
            pltpu.VMEM((12 * ny + 2 * edge, 3 * depth), bf16),
            pltpu.VMEM((3, 4, ny + 2 * edge, nz), f32),
            pltpu.VMEM((3, 2, ny, nz), f32),
            pltpu.VMEM((3 * depth, nz), bf16),
            pltpu.VMEM((3 * depth, nz), bf16),
            pltpu.VMEM((4, 6 * ny, nz), bf16),
            pltpu.VMEM((modes, 6 * ny), f32),
            dma((2,)), dma((4,)), dma((2,)),
            dma((ngz,)), dma((ngz,)), dma((ngz,)), dma((ngz,)),
            dma((2, 6)), dma((2, 6)), dma((2,)), dma((2,)),
            dma((2,)), dma((2,)), dma((2,)), dma((2,)),
        ],
        compiler_params=pltpu.CompilerParams(
            collective_id=0, has_side_effects=True, vmem_limit_bytes=52 << 20
        ),
    )(vm, conformation, tab_b, tab_s)
    stress = jnp.transpose(sout.reshape(3, nm, planes, ny), (0, 2, 3, 1))
    return out, stress


def solution(mesh):
    return jax.shard_map(
        shards,
        mesh=mesh,
        in_specs=(P(None, None, "gy", "gz"), P(None, "gz", "gy", None)),
        out_specs=(P(None, "gz", "gy", None), P(None, None, "gy", "gz")),
        check_vma=False,
    )
```

```python
import functools
import math

import jax
import jax.numpy as jnp
import ml_dtypes
import numpy as np
from jax import lax
from jax.experimental import pallas as pl
from jax.experimental.pallas import tpu as pltpu
from jax.sharding import PartitionSpec as P

max_extension = 60.0
time_step = 0.25
relax_time = 4.0
stress_scale = 0.2
component_index = ((0, 1, 2), (1, 3, 4), (2, 4, 5))
MESH = pl.DeviceIdType.MESH
edge = 8


def round_up(value, unit):
    return (value + unit - 1) // unit * unit


@functools.lru_cache
def spanwise_tables(modes, points, depth):
    half = modes // 2
    index_j = np.arange(modes, dtype=np.int64)
    index_n = np.arange(points, dtype=np.int64)
    wave = np.where(index_j < half, index_j, index_j - half + 1)
    theta = (wave[:, None] * index_n[None, :] % points) * (2.0 * math.pi / points)
    rate = wave[:, None] * (2.0 * math.pi / points)
    is_cosine = (index_j < half)[:, None]
    basis = np.where(is_cosine, np.cos(theta), np.sin(theta))
    slope = np.where(is_cosine, -rate * np.sin(theta), rate * np.cos(theta))
    tables = []
    for table in (basis, slope):
        table = np.pad(table, ((0, depth - modes), (0, 0))).astype(np.float32)
        head = table.astype(ml_dtypes.bfloat16)
        rest = (table - head.astype(np.float32)).astype(ml_dtypes.bfloat16)
        tables.append(np.concatenate([head, rest], axis=0))
    return tables


def split(value):
    head = value.astype(jnp.bfloat16)
    return head, (value - head.astype(jnp.float32)).astype(jnp.bfloat16)


def kernel(
    dims,
    vm, conf, tab_b, tab_s,
    nxt, sbuf,
    vmv, confx, fac, send, recv, osend, orecv, cols, rows, vhalo, yhalo, vedge, cedge, cnear, lhs, velx, veldz,
    tbv, tsv, pull, res,
    load_sem, tab_sem, own_sem,
    a2a_send, a2a_recv, o2a_send, o2a_recv,
    cx_send, cx_recv, cy_send, cy_recv, vx_send, vx_recv, vy_send, vy_recv,
):
    ngy, ngz, nm, ny, nz, depth = dims
    modes = nm * ngz
    gy = lax.axis_index("gy")
    gz = lax.axis_index("gz")
    right = lax.rem(gz + 1, ngz)
    left = lax.rem(gz + ngz - 1, ngz)
    has_low = gy > 0
    has_high = gy < ngy - 1
    body = slice(edge, edge + ny)
    tall = send.shape[0] // ngz
    f32 = jnp.float32
    pieces = ((0, 2 * nz // 3), (2 * nz // 3, nz // 3))

    ring = ngz // 4
    core = lax.rem(gz, 2)
    chip = lax.rem(lax.div(gz, 2), ring)
    high = lax.div(gz, 2 * ring)

    def peer_of(step, way):
        turn = lax.div(step, 4)
        hop = lax.div(turn + 1, 2) * (2 * lax.rem(turn, 2) - 1)
        return (
            lax.rem(high + lax.rem(lax.div(step, 2), 2), 2) * (2 * ring)
            + lax.rem(chip + way * hop + ring, ring) * 2
            + lax.rem(core + lax.rem(step, 2), 2)
        )

    barrier = pltpu.get_barrier_semaphore()

    def greet(step, carry):
        peer = lax.rem(gz + step, ngz)
        pl.semaphore_signal(barrier, inc=1, device_id=(gy, peer), device_id_type=MESH)
        return carry

    lax.fori_loop(1, ngz, greet, 0)

    @pl.when(has_low)
    def _():
        pl.semaphore_signal(barrier, inc=1, device_id=(gy - 1, gz), device_id_type=MESH)

    @pl.when(has_high)
    def _():
        pl.semaphore_signal(barrier, inc=1, device_id=(gy + 1, gz), device_id_type=MESH)

    load_vm = pltpu.make_async_copy(vm, vmv, load_sem.at[0])
    load_vm.start()
    load_conf = pltpu.make_async_copy(conf, confx.at[:, 1:3, body, :], load_sem.at[1])
    load_conf.start()
    table_loads = []
    for index, (source, target) in enumerate(((tab_b, tbv), (tab_s, tsv))):
        table_loads.append(
            pltpu.make_async_copy(source, target.at[0 : 2 * depth], tab_sem.at[2 * index])
        )
        table_loads.append(
            pltpu.make_async_copy(
                source.at[0:depth], target.at[2 * depth : 3 * depth], tab_sem.at[2 * index + 1]
            )
        )
    for load in table_loads:
        load.start()

    load_vm.wait()

    def pack(cm, carry):
        even = vmv[cm, pl.ds(0, ngz, stride=2), :]
        odd = vmv[cm, pl.ds(1, ngz, stride=2), :]
        send[pl.ds(cm, ngz, stride=tall), :] = jnp.concatenate([even, odd], axis=1)
        return carry

    lax.fori_loop(0, 3 * nm, pack, 0, unroll=9)

    low_count = lax.div(gy + ngy - 1, ngy)
    high_count = lax.div(2 * ngy - 2 - gy, ngy)
    pl.semaphore_wait(barrier, ngz - 1 + low_count + high_count)

    cx_up = [
        pltpu.make_async_remote_copy(
            conf.at[c, 1], confx.at[c, 0, body, :], cx_send.at[0, c], cx_recv.at[0, c],
            device_id=(gy, right), device_id_type=MESH,
        )
        for c in range(6)
    ]
    cx_down = [
        pltpu.make_async_remote_copy(
            conf.at[c, 0], confx.at[c, 3, body, :], cx_send.at[1, c], cx_recv.at[1, c],
            device_id=(gy, left), device_id_type=MESH,
        )
        for c in range(6)
    ]
    cy_up = pltpu.make_async_remote_copy(
        cedge.at[1], cnear.at[0],
        cy_send.at[0], cy_recv.at[0], device_id=(gy + 1, gz), device_id_type=MESH,
    )
    cy_down = pltpu.make_async_remote_copy(
        cedge.at[0], cnear.at[1],
        cy_send.at[1], cy_recv.at[1], device_id=(gy - 1, gz), device_id_type=MESH,
    )
    def words(source, peer):
        return source.at[pl.ds(pl.multiple_of(peer * tall, 8), 3 * nm), :]

    def message(source, target, send_sem, recv_sem, mine, theirs, peer):
        return pltpu.make_async_remote_copy(
            words(source, mine), target.at[theirs], send_sem.at[mine], recv_sem.at[theirs],
            device_id=(gy, peer), device_id_type=MESH,
        )

    def exchange_start(source, target, send_sem, recv_sem, own):
        def start(step, carry):
            peer = peer_of(step, 1)
            message(source, target, send_sem, recv_sem, peer, gz, peer).start()
            return carry

        lax.fori_loop(1, ngz, start, 0)
        pltpu.make_async_copy(words(source, gz), target.at[gz], own).start()

    def exchange_recv(source, target, send_sem, recv_sem, own, use):
        pltpu.make_async_copy(words(source, gz), target.at[gz], own).wait()
        use(gz)

        def wait(step, carry):
            peer = peer_of(step, -1)
            message(source, target, send_sem, recv_sem, peer, peer, peer).wait_recv()
            use(peer)
            return carry

        lax.fori_loop(1, ngz, wait, 0)

    def exchange_sent(source, target, send_sem, recv_sem):
        def wait(step, carry):
            peer = peer_of(step, 1)
            message(source, target, send_sem, recv_sem, peer, peer, peer).wait_send()
            return carry

        lax.fori_loop(1, ngz, wait, 0)

    exchange_start(send, recv, a2a_send, a2a_recv, own_sem.at[0])
    for c in (0, 3, 5, 1, 2):
        cx_up[c].start()
        cx_down[c].start()

    load_conf.wait()
    cedge[...] = jnp.zeros_like(cedge)
    for c in range(6):
        for p in range(2):
            at = slice(2 * c + p, 2 * c + p + 1)
            cedge[0, at, :] = confx[c, 1 + p, edge : edge + 1, :]
            cedge[1, at, :] = confx[c, 1 + p, edge + ny - 1 : edge + ny, :]

    @pl.when(has_high)
    def _():
        cy_up.start()

    @pl.when(has_low)
    def _():
        cy_down.start()

    for load in table_loads:
        load.wait()

    @pl.when(has_low)
    def _():
        cy_up.wait_recv()

    @pl.when(has_high)
    def _():
        cy_down.wait_recv()

    @pl.when(jnp.logical_not(has_low))
    def _():
        cnear[0] = jnp.zeros((16, nz), f32)

    @pl.when(jnp.logical_not(has_high))
    def _():
        cnear[1] = jnp.zeros((16, nz), f32)

    blank = jnp.zeros((edge - 1, nz), f32)
    for c in range(6):
        for p in range(2):
            at = slice(2 * c + p, 2 * c + p + 1)
            confx[c, 1 + p, 0:edge, :] = jnp.concatenate([blank, cnear[0, at, :]], axis=0)
            confx[c, 1 + p, edge + ny :, :] = jnp.concatenate([cnear[1, at, :], blank], axis=0)

    def factor_of(plane, at):
        trace = confx[0, plane, at, :] + confx[3, plane, at, :] + confx[5, plane, at, :]
        return (max_extension - 3.0) / (max_extension - trace)

    def factor_rows(block, carry):
        at = pl.ds(pl.multiple_of(block * 8, 8), 8)
        fac[0, at, :] = factor_of(1, at)
        fac[1, at, :] = factor_of(2, at)
        return carry

    lax.fori_loop(0, ny // 8 + 2, factor_rows, 0)

    weight = 2.0 / nz

    def own_rows(step, carry):
        first = pl.multiple_of(edge + step * 16, 8)
        here = pl.ds(first, 16)
        around = pl.ds(pl.multiple_of(first - 8, 8), 32)
        target = pl.ds(pl.multiple_of(step * 16, 16), 16)
        for plane in range(2):
            for row in range(3):
                cx, cy, cz = component_index[row]
                pulled = fac[plane, around, :] * confx[cy, plane + 1, around, :]
                other = fac[1 - plane, here, :] * confx[cx, 2 - plane, here, :]
                along = pulled[9:25] - pulled[7:23]
                nxt[row, plane, target, :] = along + other if plane == 0 else along - other
                spanwise = fac[plane, here, :] * confx[cz, plane + 1, here, :]
                at = pl.ds(pl.multiple_of((row * 2 + plane) * ny + step * 16, 16), 16)
                head, rest = split(spanwise * (-stress_scale * weight))
                pull[2, at, :] = head
                pull[3, at, :] = rest
        return carry

    lax.fori_loop(0, ny // 16, own_rows, 0)

    chunk = modes // 2

    def across(a, b):
        return lax.dot_general(a, b, (((1,), (1,)), ((), ())), preferred_element_type=f32)

    def project(table, which, step):
        first = pl.multiple_of(step * chunk, 16)
        head = table[pl.ds(first, chunk), :]
        rest = table[pl.ds(pl.multiple_of(depth + first, 16), chunk), :]
        total = across(head, pull[which]) + across(head, pull[which + 1])
        return total + across(rest, pull[which]), pl.ds(first, chunk)

    def project_spanwise(step, carry):
        total, at = project(tsv, 2, step)
        res[at, :] = total
        return carry

    lax.fori_loop(0, 2, project_spanwise, 0)

    for c in range(3):
        cols[c, modes:depth, :] = jnp.zeros((depth - modes, 2 * ny), f32)

    def place(k):
        for c in range(3):
            cols[c, pl.ds(k * nm, nm), :] = recv[k, c * nm : (c + 1) * nm, :]

    exchange_recv(send, recv, a2a_send, a2a_recv, own_sem.at[0], place)
    for c in range(3):
        turned = cols[c].T
        rows[c] = turned.reshape(2, ny, depth)

    vx_up = pltpu.make_async_remote_copy(
        rows.at[:, 1], vhalo.at[0], vx_send.at[0], vx_recv.at[0],
        device_id=(gy, right), device_id_type=MESH,
    )
    vx_down = pltpu.make_async_remote_copy(
        rows.at[:, 0], vhalo.at[1], vx_send.at[1], vx_recv.at[1],
        device_id=(gy, left), device_id_type=MESH,
    )
    vy_up = pltpu.make_async_remote_copy(
        vedge.at[1], yhalo.at[0], vy_send.at[0], vy_recv.at[0],
        device_id=(gy + 1, gz), device_id_type=MESH,
    )
    vy_down = pltpu.make_async_remote_copy(
        vedge.at[0], yhalo.at[1], vy_send.at[1], vy_recv.at[1],
        device_id=(gy - 1, gz), device_id_type=MESH,
    )
    vx_up.start()
    vx_down.start()
    cx_up[4].start()
    cx_down[4].start()

    vedge[...] = jnp.zeros_like(vedge)
    for c in range(3):
        for p in range(2):
            at = slice(2 * c + p, 2 * c + p + 1)
            vedge[0, at, :] = rows[c, p, 0:1, :]
            vedge[1, at, :] = rows[c, p, ny - 1 : ny, :]

    @pl.when(has_high)
    def _():
        vy_up.start()

    @pl.when(has_low)
    def _():
        vy_down.start()

    def put_lhs(first, value):
        head, rest = split(value)
        at = slice(first, first + value.shape[0])
        lhs[at, 0:depth] = head
        lhs[at, depth : 2 * depth] = head
        lhs[at, 2 * depth : 3 * depth] = rest

    for c in range(3):
        for p in range(2):
            put_lhs((c * 2 + p) * ny, rows[c, p])

    for first, wide in pieces:
        at = slice(first, first + wide)
        fine = jnp.dot(lhs[0 : 6 * ny, :], tbv[:, at], preferred_element_type=f32)
        velx[:, 1:3, body, at] = fine.reshape(3, 2, ny, wide)
        fine = jnp.dot(lhs[0 : 6 * ny, :], tsv[:, at], preferred_element_type=f32)
        veldz[:, :, :, at] = fine.reshape(3, 2, ny, wide)

    for c in (0, 3, 5, 1, 2):
        cx_up[c].wait_recv()
        cx_down[c].wait_recv()

    def halo_rows(step, carry):
        here = pl.ds(pl.multiple_of(edge + step * 16, 8), 16)
        target = pl.ds(pl.multiple_of(step * 16, 16), 16)
        for plane in range(2):
            outer = factor_of(3 * plane, here)
            for row in range(3):
                pulled = outer * confx[component_index[row][0], 3 * plane, here, :]
                along = nxt[row, plane, target, :]
                along = along - pulled if plane == 0 else along + pulled
                at = pl.ds(pl.multiple_of((row * 2 + plane) * ny + step * 16, 16), 16)
                head, rest = split(along * (0.5 * stress_scale * weight))
                pull[0, at, :] = head
                pull[1, at, :] = rest
        return carry

    lax.fori_loop(0, ny // 16, halo_rows, 0)

    def project_along(step, carry):
        total, at = project(tbv, 0, step)
        res[at, :] = res[at, :] + total
        return carry

    lax.fori_loop(0, 2, project_along, 0)
    head_row = lax.broadcasted_iota(jnp.int32, (8, 6 * ny), 0) == 0
    res[0:8, :] = jnp.where(head_row, 0.5 * res[0:8, :], res[0:8, :])
    for k in range(ngz):
        for c in range(3):
            osend[k * tall + c * nm : k * tall + (c + 1) * nm, :] = res[
                k * nm : (k + 1) * nm, c * 2 * ny : (c + 1) * 2 * ny
            ]

    vx_up.wait_recv()
    vx_down.wait_recv()
    exchange_start(osend, orecv, o2a_send, o2a_recv, own_sem.at[1])

    @pl.when(has_low)
    def _():
        vy_up.wait_recv()

    @pl.when(has_high)
    def _():
        vy_down.wait_recv()

    @pl.when(jnp.logical_not(has_low))
    def _():
        yhalo[0] = jnp.zeros((edge, depth), f32)

    @pl.when(jnp.logical_not(has_high))
    def _():
        yhalo[1] = jnp.zeros((edge, depth), f32)

    put_lhs(12 * ny, yhalo[...].reshape(2 * edge, depth))
    for side in range(2):
        for c in range(3):
            put_lhs((6 + side * 3 + c) * ny, vhalo[side, c])

    for first, wide in pieces:
        at = slice(first, first + wide)
        fine = jnp.dot(lhs[6 * ny : 12 * ny + 2 * edge, :], tbv[:, at], preferred_element_type=f32)
        velx[:, 0, body, at] = fine[0 : 3 * ny].reshape(3, ny, wide)
        velx[:, 3, body, at] = fine[3 * ny : 6 * ny].reshape(3, ny, wide)
        for c in range(3):
            for p in range(2):
                row = 6 * ny + 2 * c + p
                velx[c, 1 + p, edge - 1 : edge, at] = fine[row : row + 1]
                velx[c, 1 + p, edge + ny : edge + ny + 1, at] = fine[row + edge : row + edge + 1]

    quarter = time_step

    def update_rows(step, carry):
        plane = step // (ny // 8)
        first = pl.multiple_of(edge + (step % (ny // 8)) * 8, 8)
        here = pl.ds(first, 8)
        around = pl.ds(pl.multiple_of(first - 8, 8), 24)
        target = pl.ds(pl.multiple_of(first - edge, 8), 8)
        speed = [quarter * velx[a, plane + 1, here, :] for a in range(3)]
        plus = [jnp.maximum(s, 0.0) for s in speed]
        minus = [jnp.maximum(-s, 0.0) for s in speed]
        drain = (jnp.abs(speed[0]) + jnp.abs(speed[1])) + jnp.abs(speed[2])
        keep = (1.0 - drain) - (time_step / relax_time) * fac[plane, here, :]
        centre = [confx[c, plane + 1, here, :] for c in range(6)]
        grown = []
        for a in range(3):
            tall = velx[a, plane + 1, around, :]
            grad = (
                (0.5 * quarter) * (velx[a, plane + 2, here, :] - velx[a, plane, here, :]),
                (0.5 * quarter) * (tall[9:17] - tall[7:15]),
                quarter * veldz[a, plane, target, :],
            )
            grown.append(
                [
                    (grad[0] * centre[component_index[0][b]] + grad[1] * centre[component_index[1][b]])
                    + grad[2] * centre[component_index[2][b]]
                    for b in range(3)
                ]
            )
        for c, (a, b) in enumerate(((0, 0), (0, 1), (0, 2), (1, 1), (1, 2), (2, 2))):
            tall = confx[c, plane + 1, around, :]
            total = grown[a][b] + grown[b][a]
            total = total + keep * centre[c]
            total = total + plus[0] * confx[c, plane, here, :]
            total = total + minus[0] * confx[c, plane + 2, here, :]
            total = total + plus[1] * tall[7:15]
            total = total + minus[1] * tall[9:17]
            total = total + plus[2] * pltpu.roll(centre[c], 1, 1)
            total = total + minus[2] * pltpu.roll(centre[c], nz - 1, 1)
            if a == b:
                total = total + time_step / relax_time
            nxt[c, plane, target, :] = total
        return carry

    cx_up[4].wait_recv()
    cx_down[4].wait_recv()
    lax.fori_loop(0, 2 * (ny // 8), update_rows, 0)

    def unpack(k):
        pair = orecv[k]
        sbuf[pl.ds(2 * k, 3 * nm, stride=2 * ngz), :] = pair[:, 0:ny]
        sbuf[pl.ds(2 * k + 1, 3 * nm, stride=2 * ngz), :] = pair[:, ny : 2 * ny]

    exchange_recv(osend, orecv, o2a_send, o2a_recv, own_sem.at[1], unpack)

    exchange_sent(send, recv, a2a_send, a2a_recv)
    exchange_sent(osend, orecv, o2a_send, o2a_recv)
    for c in range(6):
        cx_up[c].wait_send()
        cx_down[c].wait_send()
    vx_up.wait_send()
    vx_down.wait_send()

    @pl.when(has_high)
    def _():
        cy_up.wait_send()
        vy_up.wait_send()

    @pl.when(has_low)
    def _():
        cy_down.wait_send()
        vy_down.wait_send()


def shards(velocity_modes, conformation):
    ngy = lax.axis_size("gy")
    ngz = lax.axis_size("gz")
    _, planes, ny, nm = velocity_modes.shape
    nz = conformation.shape[3]
    modes = nm * ngz
    depth = round_up(modes, 128)
    tab_b, tab_s = (jnp.asarray(t) for t in spanwise_tables(modes, nz, depth))
    vm = jnp.transpose(velocity_modes, (0, 3, 1, 2)).reshape(3 * nm, planes, ny)
    f32, bf16 = jnp.float32, jnp.bfloat16
    dma = pltpu.SemaphoreType.DMA
    anywhere = pl.BlockSpec(memory_space=pl.ANY)
    out, sout = pl.pallas_call(
        functools.partial(kernel, (ngy, ngz, nm, ny, nz, depth)),
        name="fene_step",
        out_shape=(
            pltpu.VMEM(conformation.shape, f32),
            pltpu.VMEM((3 * nm * planes, ny), f32),
        ),
        in_specs=[anywhere] * 4,
        out_specs=[pl.BlockSpec(memory_space=pltpu.VMEM)] * 2,
        scratch_shapes=[
            pltpu.VMEM((3 * nm, planes, ny), f32),
            pltpu.VMEM((6, 4, ny + 2 * edge, nz), f32),
            pltpu.VMEM((2, ny + 2 * edge, nz), f32),
            pltpu.VMEM((ngz * round_up(3 * nm, 8), 2 * ny), f32),
            pltpu.VMEM((ngz, 3 * nm, 2 * ny), f32),
            pltpu.VMEM((ngz * round_up(3 * nm, 8), 2 * ny), f32),
            pltpu.VMEM((ngz, 3 * nm, 2 * ny), f32),
            pltpu.VMEM((3, depth, 2 * ny), f32),
            pltpu.VMEM((3, 2, ny, depth), f32),
            pltpu.VMEM((2, 3, ny, depth), f32),
            pltpu.VMEM((2, edge, depth), f32),
            pltpu.VMEM((2, edge, depth), f32),
            pltpu.VMEM((2, 16, nz), f32),
            pltpu.VMEM((2, 16, nz), f32),
            pltpu.VMEM((12 * ny + 2 * edge, 3 * depth), bf16),
            pltpu.VMEM((3, 4, ny + 2 * edge, nz), f32),
            pltpu.VMEM((3, 2, ny, nz), f32),
            pltpu.VMEM((3 * depth, nz), bf16),
            pltpu.VMEM((3 * depth, nz), bf16),
            pltpu.VMEM((4, 6 * ny, nz), bf16),
            pltpu.VMEM((modes, 6 * ny), f32),
            dma((2,)), dma((4,)), dma((2,)),
            dma((ngz,)), dma((ngz,)), dma((ngz,)), dma((ngz,)),
            dma((2, 6)), dma((2, 6)), dma((2,)), dma((2,)),
            dma((2,)), dma((2,)), dma((2,)), dma((2,)),
        ],
        compiler_params=pltpu.CompilerParams(
            collective_id=0, has_side_effects=True, vmem_limit_bytes=52 << 20
        ),
    )(vm, conformation, tab_b, tab_s)
    stress = jnp.transpose(sout.reshape(3, nm, planes, ny), (0, 2, 3, 1))
    return out, stress


def solution(mesh):
    return jax.shard_map(
        shards,
        mesh=mesh,
        in_specs=(P(None, None, "gy", "gz"), P(None, "gz", "gy", None)),
        out_specs=(P(None, "gz", "gy", None), P(None, None, "gy", "gz")),
        check_vma=False,
    )
```

```python
import functools
import math

import jax
import jax.numpy as jnp
import ml_dtypes
import numpy as np
from jax import lax
from jax.experimental import pallas as pl
from jax.experimental.pallas import tpu as pltpu
from jax.sharding import PartitionSpec as P

max_extension = 60.0
time_step = 0.25
relax_time = 4.0
stress_scale = 0.2
component_index = ((0, 1, 2), (1, 3, 4), (2, 4, 5))
MESH = pl.DeviceIdType.MESH
edge = 8


def round_up(value, unit):
    return (value + unit - 1) // unit * unit


@functools.lru_cache
def spanwise_tables(modes, points, depth):
    half = modes // 2
    index_j = np.arange(modes, dtype=np.int64)
    index_n = np.arange(points, dtype=np.int64)
    wave = np.where(index_j < half, index_j, index_j - half + 1)
    theta = (wave[:, None] * index_n[None, :] % points) * (2.0 * math.pi / points)
    rate = wave[:, None] * (2.0 * math.pi / points)
    is_cosine = (index_j < half)[:, None]
    basis = np.where(is_cosine, np.cos(theta), np.sin(theta))
    slope = np.where(is_cosine, -rate * np.sin(theta), rate * np.cos(theta))
    tables = []
    for table in (basis, slope):
        table = np.pad(table, ((0, depth - modes), (0, 0))).astype(np.float32)
        head = table.astype(ml_dtypes.bfloat16)
        rest = (table - head.astype(np.float32)).astype(ml_dtypes.bfloat16)
        tables.append(np.concatenate([head, rest], axis=0))
    return tables


def split(value):
    head = value.astype(jnp.bfloat16)
    return head, (value - head.astype(jnp.float32)).astype(jnp.bfloat16)


def kernel(
    dims,
    vm, conf, tab_b, tab_s,
    nxt, sbuf,
    vmv, confx, fac, send, recv, osend, orecv, cols, rows, vhalo, yhalo, vedge, cedge, cnear, lhs, velx, veldz,
    tbv, tsv, pull, res,
    load_sem, tab_sem, own_sem,
    a2a_send, a2a_recv, o2a_send, o2a_recv,
    cx_send, cx_recv, cy_send, cy_recv, vx_send, vx_recv, vy_send, vy_recv,
):
    ngy, ngz, nm, ny, nz, depth = dims
    modes = nm * ngz
    gy = lax.axis_index("gy")
    gz = lax.axis_index("gz")
    right = lax.rem(gz + 1, ngz)
    left = lax.rem(gz + ngz - 1, ngz)
    has_low = gy > 0
    has_high = gy < ngy - 1
    body = slice(edge, edge + ny)
    tall = send.shape[0] // ngz
    f32 = jnp.float32
    pieces = ((0, 2 * nz // 3), (2 * nz // 3, nz // 3))

    ring = ngz // 4
    core = lax.rem(gz, 2)
    chip = lax.rem(lax.div(gz, 2), ring)
    high = lax.div(gz, 2 * ring)

    def peer_of(step, way):
        turn = lax.div(step, 4)
        hop = lax.div(turn + 1, 2) * (2 * lax.rem(turn, 2) - 1)
        return (
            lax.rem(high + lax.rem(lax.div(step, 2), 2), 2) * (2 * ring)
            + lax.rem(chip + way * hop + ring, ring) * 2
            + lax.rem(core + lax.rem(step, 2), 2)
        )

    barrier = pltpu.get_barrier_semaphore()

    def greet(step, carry):
        peer = lax.rem(gz + step, ngz)
        pl.semaphore_signal(barrier, inc=1, device_id=(gy, peer), device_id_type=MESH)
        return carry

    lax.fori_loop(1, ngz, greet, 0)

    @pl.when(has_low)
    def _():
        pl.semaphore_signal(barrier, inc=1, device_id=(gy - 1, gz), device_id_type=MESH)

    @pl.when(has_high)
    def _():
        pl.semaphore_signal(barrier, inc=1, device_id=(gy + 1, gz), device_id_type=MESH)

    load_vm = pltpu.make_async_copy(vm, vmv, load_sem.at[0])
    load_vm.start()
    load_conf = pltpu.make_async_copy(conf, confx.at[:, 1:3, body, :], load_sem.at[1])
    load_conf.start()
    table_loads = []
    for index, (source, target) in enumerate(((tab_b, tbv), (tab_s, tsv))):
        table_loads.append(
            pltpu.make_async_copy(source, target.at[0 : 2 * depth], tab_sem.at[2 * index])
        )
        table_loads.append(
            pltpu.make_async_copy(
                source.at[0:depth], target.at[2 * depth : 3 * depth], tab_sem.at[2 * index + 1]
            )
        )
    for load in table_loads:
        load.start()

    load_vm.wait()

    def pack(cm, carry):
        even = vmv[cm, pl.ds(0, ngz, stride=2), :]
        odd = vmv[cm, pl.ds(1, ngz, stride=2), :]
        send[pl.ds(cm, ngz, stride=tall), :] = jnp.concatenate([even, odd], axis=1)
        return carry

    lax.fori_loop(0, 3 * nm, pack, 0, unroll=9)

    low_count = lax.div(gy + ngy - 1, ngy)
    high_count = lax.div(2 * ngy - 2 - gy, ngy)
    pl.semaphore_wait(barrier, ngz - 1 + low_count + high_count)

    cx_up = [
        pltpu.make_async_remote_copy(
            conf.at[c, 1], confx.at[c, 0, body, :], cx_send.at[0, c], cx_recv.at[0, c],
            device_id=(gy, right), device_id_type=MESH,
        )
        for c in range(6)
    ]
    cx_down = [
        pltpu.make_async_remote_copy(
            conf.at[c, 0], confx.at[c, 3, body, :], cx_send.at[1, c], cx_recv.at[1, c],
            device_id=(gy, left), device_id_type=MESH,
        )
        for c in range(6)
    ]
    cy_up = pltpu.make_async_remote_copy(
        cedge.at[1], cnear.at[0],
        cy_send.at[0], cy_recv.at[0], device_id=(gy + 1, gz), device_id_type=MESH,
    )
    cy_down = pltpu.make_async_remote_copy(
        cedge.at[0], cnear.at[1],
        cy_send.at[1], cy_recv.at[1], device_id=(gy - 1, gz), device_id_type=MESH,
    )
    def words(source, peer):
        return source.at[pl.ds(pl.multiple_of(peer * tall, 8), 3 * nm), :]

    def message(source, target, send_sem, recv_sem, mine, theirs, peer):
        return pltpu.make_async_remote_copy(
            words(source, mine), target.at[theirs], send_sem.at[mine], recv_sem.at[theirs],
            device_id=(gy, peer), device_id_type=MESH,
        )

    def exchange_start(source, target, send_sem, recv_sem, own):
        def start(step, carry):
            peer = peer_of(step, 1)
            message(source, target, send_sem, recv_sem, peer, gz, peer).start()
            return carry

        lax.fori_loop(1, ngz, start, 0)
        pltpu.make_async_copy(words(source, gz), target.at[gz], own).start()

    def exchange_recv(source, target, send_sem, recv_sem, own, use):
        pltpu.make_async_copy(words(source, gz), target.at[gz], own).wait()
        use(gz)

        def wait(step, carry):
            peer = peer_of(step, -1)
            message(source, target, send_sem, recv_sem, peer, peer, peer).wait_recv()
            use(peer)
            return carry

        lax.fori_loop(1, ngz, wait, 0)

    def exchange_sent(source, target, send_sem, recv_sem):
        def wait(step, carry):
            peer = peer_of(step, 1)
            message(source, target, send_sem, recv_sem, peer, peer, peer).wait_send()
            return carry

        lax.fori_loop(1, ngz, wait, 0)

    exchange_start(send, recv, a2a_send, a2a_recv, own_sem.at[0])
    for c in (0, 3, 5, 1, 2):
        cx_up[c].start()
        cx_down[c].start()

    load_conf.wait()
    cedge[...] = jnp.zeros_like(cedge)
    for c in range(6):
        for p in range(2):
            at = slice(2 * c + p, 2 * c + p + 1)
            cedge[0, at, :] = confx[c, 1 + p, edge : edge + 1, :]
            cedge[1, at, :] = confx[c, 1 + p, edge + ny - 1 : edge + ny, :]

    @pl.when(has_high)
    def _():
        cy_up.start()

    @pl.when(has_low)
    def _():
        cy_down.start()

    for load in table_loads:
        load.wait()

    @pl.when(has_low)
    def _():
        cy_up.wait_recv()

    @pl.when(has_high)
    def _():
        cy_down.wait_recv()

    @pl.when(jnp.logical_not(has_low))
    def _():
        cnear[0] = jnp.zeros((16, nz), f32)

    @pl.when(jnp.logical_not(has_high))
    def _():
        cnear[1] = jnp.zeros((16, nz), f32)

    blank = jnp.zeros((edge - 1, nz), f32)
    for c in range(6):
        for p in range(2):
            at = slice(2 * c + p, 2 * c + p + 1)
            confx[c, 1 + p, 0:edge, :] = jnp.concatenate([blank, cnear[0, at, :]], axis=0)
            confx[c, 1 + p, edge + ny :, :] = jnp.concatenate([cnear[1, at, :], blank], axis=0)

    def factor_of(plane, at):
        trace = confx[0, plane, at, :] + confx[3, plane, at, :] + confx[5, plane, at, :]
        return (max_extension - 3.0) / (max_extension - trace)

    def factor_rows(block, carry):
        at = pl.ds(pl.multiple_of(block * 8, 8), 8)
        fac[0, at, :] = factor_of(1, at)
        fac[1, at, :] = factor_of(2, at)
        return carry

    lax.fori_loop(0, ny // 8 + 2, factor_rows, 0)

    weight = 2.0 / nz

    def own_rows(step, carry):
        first = pl.multiple_of(edge + step * 16, 8)
        here = pl.ds(first, 16)
        around = pl.ds(pl.multiple_of(first - 8, 8), 32)
        target = pl.ds(pl.multiple_of(step * 16, 16), 16)
        for plane in range(2):
            for row in range(3):
                cx, cy, cz = component_index[row]
                pulled = fac[plane, around, :] * confx[cy, plane + 1, around, :]
                other = fac[1 - plane, here, :] * confx[cx, 2 - plane, here, :]
                along = pulled[9:25] - pulled[7:23]
                nxt[row, plane, target, :] = along + other if plane == 0 else along - other
                spanwise = fac[plane, here, :] * confx[cz, plane + 1, here, :]
                at = pl.ds(pl.multiple_of((row * 2 + plane) * ny + step * 16, 16), 16)
                head, rest = split(spanwise * (-stress_scale * weight))
                pull[2, at, :] = head
                pull[3, at, :] = rest
        return carry

    lax.fori_loop(0, ny // 16, own_rows, 0)

    chunk = modes // 2

    def across(a, b):
        return lax.dot_general(a, b, (((1,), (1,)), ((), ())), preferred_element_type=f32)

    def project(table, which, step):
        first = pl.multiple_of(step * chunk, 16)
        head = table[pl.ds(first, chunk), :]
        rest = table[pl.ds(pl.multiple_of(depth + first, 16), chunk), :]
        total = across(head, pull[which]) + across(head, pull[which + 1])
        return total + across(rest, pull[which]), pl.ds(first, chunk)

    def project_spanwise(step, carry):
        total, at = project(tsv, 2, step)
        res[at, :] = total
        return carry

    lax.fori_loop(0, 2, project_spanwise, 0)

    for c in range(3):
        cols[c, modes:depth, :] = jnp.zeros((depth - modes, 2 * ny), f32)

    def place(k):
        for c in range(3):
            cols[c, pl.ds(k * nm, nm), :] = recv[k, c * nm : (c + 1) * nm, :]

    exchange_recv(send, recv, a2a_send, a2a_recv, own_sem.at[0], place)
    vx_up = [
        pltpu.make_async_remote_copy(
            rows.at[c, 1], vhalo.at[0, c], vx_send.at[0, c], vx_recv.at[0, c],
            device_id=(gy, right), device_id_type=MESH,
        )
        for c in range(3)
    ]
    vx_down = [
        pltpu.make_async_remote_copy(
            rows.at[c, 0], vhalo.at[1, c], vx_send.at[1, c], vx_recv.at[1, c],
            device_id=(gy, left), device_id_type=MESH,
        )
        for c in range(3)
    ]
    for c in range(3):
        turned = cols[c].T
        rows[c] = turned.reshape(2, ny, depth)
        vx_up[c].start()
        vx_down[c].start()

    vy_up = pltpu.make_async_remote_copy(
        vedge.at[1], yhalo.at[0], vy_send.at[0], vy_recv.at[0],
        device_id=(gy + 1, gz), device_id_type=MESH,
    )
    vy_down = pltpu.make_async_remote_copy(
        vedge.at[0], yhalo.at[1], vy_send.at[1], vy_recv.at[1],
        device_id=(gy - 1, gz), device_id_type=MESH,
    )
    cx_up[4].start()
    cx_down[4].start()

    vedge[...] = jnp.zeros_like(vedge)
    for c in range(3):
        for p in range(2):
            at = slice(2 * c + p, 2 * c + p + 1)
            vedge[0, at, :] = rows[c, p, 0:1, :]
            vedge[1, at, :] = rows[c, p, ny - 1 : ny, :]

    @pl.when(has_high)
    def _():
        vy_up.start()

    @pl.when(has_low)
    def _():
        vy_down.start()

    def put_lhs(first, value):
        head, rest = split(value)
        at = slice(first, first + value.shape[0])
        lhs[at, 0:depth] = head
        lhs[at, depth : 2 * depth] = head
        lhs[at, 2 * depth : 3 * depth] = rest

    for c in range(3):
        for p in range(2):
            put_lhs((c * 2 + p) * ny, rows[c, p])

    for first, wide in pieces:
        at = slice(first, first + wide)
        fine = jnp.dot(lhs[0 : 6 * ny, :], tbv[:, at], preferred_element_type=f32)
        velx[:, 1:3, body, at] = fine.reshape(3, 2, ny, wide)
        fine = jnp.dot(lhs[0 : 6 * ny, :], tsv[:, at], preferred_element_type=f32)
        veldz[:, :, :, at] = fine.reshape(3, 2, ny, wide)

    for c in (0, 3, 5, 1, 2):
        cx_up[c].wait_recv()
        cx_down[c].wait_recv()

    def halo_rows(step, carry):
        here = pl.ds(pl.multiple_of(edge + step * 16, 8), 16)
        target = pl.ds(pl.multiple_of(step * 16, 16), 16)
        for plane in range(2):
            outer = factor_of(3 * plane, here)
            for row in range(3):
                pulled = outer * confx[component_index[row][0], 3 * plane, here, :]
                along = nxt[row, plane, target, :]
                along = along - pulled if plane == 0 else along + pulled
                at = pl.ds(pl.multiple_of((row * 2 + plane) * ny + step * 16, 16), 16)
                head, rest = split(along * (0.5 * stress_scale * weight))
                pull[0, at, :] = head
                pull[1, at, :] = rest
        return carry

    lax.fori_loop(0, ny // 16, halo_rows, 0)

    def project_along(step, carry):
        total, at = project(tbv, 0, step)
        res[at, :] = res[at, :] + total
        return carry

    lax.fori_loop(0, 2, project_along, 0)
    head_row = lax.broadcasted_iota(jnp.int32, (8, 6 * ny), 0) == 0
    res[0:8, :] = jnp.where(head_row, 0.5 * res[0:8, :], res[0:8, :])
    for k in range(ngz):
        for c in range(3):
            osend[k * tall + c * nm : k * tall + (c + 1) * nm, :] = res[
                k * nm : (k + 1) * nm, c * 2 * ny : (c + 1) * 2 * ny
            ]

    for c in range(3):
        vx_up[c].wait_recv()
        vx_down[c].wait_recv()
    exchange_start(osend, orecv, o2a_send, o2a_recv, own_sem.at[1])

    @pl.when(has_low)
    def _():
        vy_up.wait_recv()

    @pl.when(has_high)
    def _():
        vy_down.wait_recv()

    @pl.when(jnp.logical_not(has_low))
    def _():
        yhalo[0] = jnp.zeros((edge, depth), f32)

    @pl.when(jnp.logical_not(has_high))
    def _():
        yhalo[1] = jnp.zeros((edge, depth), f32)

    put_lhs(12 * ny, yhalo[...].reshape(2 * edge, depth))
    for side in range(2):
        for c in range(3):
            put_lhs((6 + side * 3 + c) * ny, vhalo[side, c])

    for first, wide in pieces:
        at = slice(first, first + wide)
        fine = jnp.dot(lhs[6 * ny : 12 * ny + 2 * edge, :], tbv[:, at], preferred_element_type=f32)
        velx[:, 0, body, at] = fine[0 : 3 * ny].reshape(3, ny, wide)
        velx[:, 3, body, at] = fine[3 * ny : 6 * ny].reshape(3, ny, wide)
        for c in range(3):
            for p in range(2):
                row = 6 * ny + 2 * c + p
                velx[c, 1 + p, edge - 1 : edge, at] = fine[row : row + 1]
                velx[c, 1 + p, edge + ny : edge + ny + 1, at] = fine[row + edge : row + edge + 1]

    quarter = time_step

    def update_rows(step, carry):
        plane = step // (ny // 8)
        first = pl.multiple_of(edge + (step % (ny // 8)) * 8, 8)
        here = pl.ds(first, 8)
        around = pl.ds(pl.multiple_of(first - 8, 8), 24)
        target = pl.ds(pl.multiple_of(first - edge, 8), 8)
        speed = [quarter * velx[a, plane + 1, here, :] for a in range(3)]
        plus = [jnp.maximum(s, 0.0) for s in speed]
        minus = [jnp.maximum(-s, 0.0) for s in speed]
        drain = (jnp.abs(speed[0]) + jnp.abs(speed[1])) + jnp.abs(speed[2])
        keep = (1.0 - drain) - (time_step / relax_time) * fac[plane, here, :]
        centre = [confx[c, plane + 1, here, :] for c in range(6)]
        grown = []
        for a in range(3):
            tall = velx[a, plane + 1, around, :]
            grad = (
                (0.5 * quarter) * (velx[a, plane + 2, here, :] - velx[a, plane, here, :]),
                (0.5 * quarter) * (tall[9:17] - tall[7:15]),
                quarter * veldz[a, plane, target, :],
            )
            grown.append(
                [
                    (grad[0] * centre[component_index[0][b]] + grad[1] * centre[component_index[1][b]])
                    + grad[2] * centre[component_index[2][b]]
                    for b in range(3)
                ]
            )
        for c, (a, b) in enumerate(((0, 0), (0, 1), (0, 2), (1, 1), (1, 2), (2, 2))):
            tall = confx[c, plane + 1, around, :]
            total = grown[a][b] + grown[b][a]
            total = total + keep * centre[c]
            total = total + plus[0] * confx[c, plane, here, :]
            total = total + minus[0] * confx[c, plane + 2, here, :]
            total = total + plus[1] * tall[7:15]
            total = total + minus[1] * tall[9:17]
            total = total + plus[2] * pltpu.roll(centre[c], 1, 1)
            total = total + minus[2] * pltpu.roll(centre[c], nz - 1, 1)
            if a == b:
                total = total + time_step / relax_time
            nxt[c, plane, target, :] = total
        return carry

    cx_up[4].wait_recv()
    cx_down[4].wait_recv()
    lax.fori_loop(0, 2 * (ny // 8), update_rows, 0)

    def unpack(k):
        pair = orecv[k]
        sbuf[pl.ds(2 * k, 3 * nm, stride=2 * ngz), :] = pair[:, 0:ny]
        sbuf[pl.ds(2 * k + 1, 3 * nm, stride=2 * ngz), :] = pair[:, ny : 2 * ny]

    exchange_recv(osend, orecv, o2a_send, o2a_recv, own_sem.at[1], unpack)

    exchange_sent(send, recv, a2a_send, a2a_recv)
    exchange_sent(osend, orecv, o2a_send, o2a_recv)
    for c in range(6):
        cx_up[c].wait_send()
        cx_down[c].wait_send()
    for c in range(3):
        vx_up[c].wait_send()
        vx_down[c].wait_send()

    @pl.when(has_high)
    def _():
        cy_up.wait_send()
        vy_up.wait_send()

    @pl.when(has_low)
    def _():
        cy_down.wait_send()
        vy_down.wait_send()


def shards(velocity_modes, conformation):
    ngy = lax.axis_size("gy")
    ngz = lax.axis_size("gz")
    _, planes, ny, nm = velocity_modes.shape
    nz = conformation.shape[3]
    modes = nm * ngz
    depth = round_up(modes, 128)
    tab_b, tab_s = (jnp.asarray(t) for t in spanwise_tables(modes, nz, depth))
    vm = jnp.transpose(velocity_modes, (0, 3, 1, 2)).reshape(3 * nm, planes, ny)
    f32, bf16 = jnp.float32, jnp.bfloat16
    dma = pltpu.SemaphoreType.DMA
    anywhere = pl.BlockSpec(memory_space=pl.ANY)
    out, sout = pl.pallas_call(
        functools.partial(kernel, (ngy, ngz, nm, ny, nz, depth)),
        name="fene_step",
        out_shape=(
            pltpu.VMEM(conformation.shape, f32),
            pltpu.VMEM((3 * nm * planes, ny), f32),
        ),
        in_specs=[anywhere] * 4,
        out_specs=[pl.BlockSpec(memory_space=pltpu.VMEM)] * 2,
        scratch_shapes=[
            pltpu.VMEM((3 * nm, planes, ny), f32),
            pltpu.VMEM((6, 4, ny + 2 * edge, nz), f32),
            pltpu.VMEM((2, ny + 2 * edge, nz), f32),
            pltpu.VMEM((ngz * round_up(3 * nm, 8), 2 * ny), f32),
            pltpu.VMEM((ngz, 3 * nm, 2 * ny), f32),
            pltpu.VMEM((ngz * round_up(3 * nm, 8), 2 * ny), f32),
            pltpu.VMEM((ngz, 3 * nm, 2 * ny), f32),
            pltpu.VMEM((3, depth, 2 * ny), f32),
            pltpu.VMEM((3, 2, ny, depth), f32),
            pltpu.VMEM((2, 3, ny, depth), f32),
            pltpu.VMEM((2, edge, depth), f32),
            pltpu.VMEM((2, edge, depth), f32),
            pltpu.VMEM((2, 16, nz), f32),
            pltpu.VMEM((2, 16, nz), f32),
            pltpu.VMEM((12 * ny + 2 * edge, 3 * depth), bf16),
            pltpu.VMEM((3, 4, ny + 2 * edge, nz), f32),
            pltpu.VMEM((3, 2, ny, nz), f32),
            pltpu.VMEM((3 * depth, nz), bf16),
            pltpu.VMEM((3 * depth, nz), bf16),
            pltpu.VMEM((4, 6 * ny, nz), bf16),
            pltpu.VMEM((modes, 6 * ny), f32),
            dma((2,)), dma((4,)), dma((2,)),
            dma((ngz,)), dma((ngz,)), dma((ngz,)), dma((ngz,)),
            dma((2, 6)), dma((2, 6)), dma((2,)), dma((2,)),
            dma((2, 3)), dma((2, 3)), dma((2,)), dma((2,)),
        ],
        compiler_params=pltpu.CompilerParams(
            collective_id=0, has_side_effects=True, vmem_limit_bytes=52 << 20
        ),
    )(vm, conformation, tab_b, tab_s)
    stress = jnp.transpose(sout.reshape(3, nm, planes, ny), (0, 2, 3, 1))
    return out, stress


def solution(mesh):
    return jax.shard_map(
        shards,
        mesh=mesh,
        in_specs=(P(None, None, "gy", "gz"), P(None, "gz", "gy", None)),
        out_specs=(P(None, "gz", "gy", None), P(None, None, "gy", "gz")),
        check_vma=False,
    )
```
